256 devices in a mesh: seq: 32 (over y, x, core), head: 8 (over z).
Axes of the slice: x: 4, y: 4, z: 8, core: 2. Of those that a mesh axis runs over, the one named last changes fastest.
Arguments:
- queries: bfloat16 [16384, 2048], P('seq', 'head'), may hold values from -60 to 60
- keys: bfloat16 [16384, 2048], P('seq', 'head'), may hold values from -6 to 6
- values: bfloat16 [16384, 2048], P('seq', 'head'), may hold values from -6 to 6
- grad_out: bfloat16 [16384, 2048], P('seq', 'head'), may hold values from -6 to 6
- retrieved: int32 [256, 16], P(('seq', 'head')), may hold values from 0 to 255, as said below
- mem_bias: float32 [16], P('head'), may hold values from -2 to 1
Outputs:
- attended: bfloat16 [16384, 2048], P('seq', 'head')
- grad_queries: bfloat16 [16384, 2048], P('seq', 'head')
- grad_keys: bfloat16 [16384, 2048], P('seq', 'head')
- grad_values: bfloat16 [16384, 2048], P('seq', 'head')
The draws below stay inside these ranges and needn't reach their ends.
Inputs may be any that keep to these rules, and one draw needn't show every extreme that they name: `retrieved`: each row names 16 different blocks. The 8 rows of one segment name exactly 32 distinct blocks together, at most 2 of them from the blocks of any one segment, and exactly 2 from some segment.
All inputs are finite; a program needn't handle non-finite values.
Results may differ from the reference program's by a relative error of at most 0.0055.
Values may be sent and summed in bfloat16 or wider, within the bound.
No kernel may reach another device: no remote copies, remote signals or barrier semaphores. Data moves between devices by JAX's collectives and lax.ppermute only.
A program may use at most 128 MiB of HBM per device.

```python
import math
import jax
import jax.numpy as jnp
from jax import lax

H = 16
HD = 128
BLK = 64
TOPK = 16
POOL = 32
TOK_DEV = 512
BLK_DEV = 8
TOKENS = 16384
NBLK = 256
CAP = 2
N_SEQ = 32


def query_key_pair(key):
    array_shape = (TOKENS, H * HD)
    key_field = jnp.clip(jax.random.normal(jax.random.fold_in(key, 31), array_shape, jnp.float32), -6.0, 6.0)
    query_field = jnp.clip(jax.random.normal(jax.random.fold_in(key, 32), array_shape, jnp.float32), -6.0, 6.0)
    return (query_field, key_field)


def draw_queries(key, part):
    return query_key_pair(key)[0].astype(jnp.bfloat16)


def draw_keys(key, part):
    return query_key_pair(key)[1].astype(jnp.bfloat16)


def draw_retrieved(key, part):
    writers = NBLK // BLK_DEV
    writer_heat = jax.random.randint(jax.random.fold_in(key, 21), (writers,), 0, 4)
    top_writer = jax.random.randint(jax.random.fold_in(key, 22), (), 0, writers)

    def one_segment(device_key):
        first_key, second_key, third_key, fourth_key = jax.random.split(device_key, 4)
        inner_pick = jax.vmap(lambda subkey: jax.random.permutation(subkey, BLK_DEV)[:CAP])(jax.random.split(first_key, writers))
        candidates = jnp.arange(writers, dtype=jnp.int32)[:, None] * BLK_DEV + inner_pick.astype(jnp.int32)
        int_noise = jax.random.randint(second_key, (writers, CAP), 0, 4)
        forced = (jnp.arange(writers, dtype=jnp.int32) == top_writer).astype(jnp.int32)[:, None] * 64
        tie_break = jax.random.permutation(third_key, writers * CAP).astype(jnp.int32).reshape(writers, CAP)
        pool_score = (int_noise + writer_heat[:, None] + forced) * (writers * CAP) + tie_break
        _, selected = lax.top_k(pool_score.reshape(-1), POOL)
        pool_blocks = candidates.reshape(-1)[selected]
        owner_row = jnp.arange(POOL, dtype=jnp.int32) % BLK_DEV
        row_ranks = jax.vmap(lambda subkey: jax.random.permutation(subkey, POOL))(jax.random.split(fourth_key, BLK_DEV)).astype(jnp.int32)
        owned = (owner_row[None, :] == jnp.arange(BLK_DEV, dtype=jnp.int32)[:, None]).astype(jnp.int32)
        _, chosen = lax.top_k(owned * POOL + row_ranks, TOPK)
        return pool_blocks[chosen]
    block_ids = jax.vmap(one_segment)(jax.random.split(key, writers))
    return block_ids.reshape(NBLK, TOPK).astype(jnp.int32)


def block_levels(key, shape, shards, least, largest):
    factor_of = 1.0
    for dim, blocks in shards:
        heights = jax.random.uniform(jax.random.fold_in(jax.random.fold_in(key, 6), dim), (blocks,), jnp.float32, least / len(shards), largest / len(shards))
        factor_of = factor_of * jnp.repeat(jnp.exp(heights), shape[dim] // blocks).reshape((-1,) + (1,) * (len(shape) - 1 - dim))
    return factor_of


def bell_draw(stream_key, extent, scale, bound, cuts=(), kind=jnp.bfloat16):
    loudness = block_levels(stream_key, extent, cuts, -0.22, 0.18) if cuts else 1.0
    values = jax.random.normal(stream_key, extent, jnp.float32) * scale * loudness
    return jnp.minimum(jnp.maximum(values, -bound), bound).astype(kind)


def setup_inputs(seed: int = 0) -> dict:
    seeds = jax.random.split(jax.random.key(seed), 7)
    return {
        "queries": draw_queries(jax.random.fold_in(seeds[6], 71), 0),
        "keys": draw_keys(jax.random.fold_in(seeds[6], 71), 0),
        "values": bell_draw(seeds[2], (TOKENS, H * HD), 1.0, 6.0, ((0, 32), (1, 8))),
        "grad_out": bell_draw(seeds[3], (TOKENS, H * HD), 1.0, 6.0, ((0, 32), (1, 8))),
        "retrieved": draw_retrieved(jax.random.fold_in(seeds[6], 71), 0),
        "mem_bias": jnp.clip(-2.0 + 3.0 * jax.random.uniform(seeds[5], (H,), jnp.float32) ** block_levels(seeds[5], (H,), ((0, 8),), -0.2, 0.2), -2.0, 1.0),
    }


def product(pattern, former, latter):
    return jnp.einsum(pattern, former.astype(jnp.float32), latter.astype(jnp.float32))

def attend_group(queries, grads, seg_keys, seg_values, mem_keys, mem_values, usable, bias, first_row):
    row_count, features = queries.shape
    head_count = bias.shape[0]
    head_size = features // head_count
    block_count, top_count, block_len, _ = mem_keys.shape
    seg_len = seg_keys.shape[0]
    score_scale = 1.0 / math.sqrt(head_size)
    query_heads = queries.reshape(block_count, block_len, head_count, head_size)
    grad_heads = grads.reshape(block_count, block_len, head_count, head_size)
    key_heads = seg_keys.reshape(seg_len, head_count, head_size)
    value_heads = seg_values.reshape(seg_len, head_count, head_size)
    mem_key_heads = mem_keys.reshape(block_count, top_count * block_len, head_count, head_size)
    mem_value_heads = mem_values.reshape(block_count, top_count * block_len, head_count, head_size)
    query_pos = first_row + jnp.arange(row_count, dtype=jnp.int32).reshape(block_count, 1, block_len, 1)
    key_pos = jnp.arange(seg_len, dtype=jnp.int32)
    local_ok = key_pos[None, None, None, :] <= query_pos
    memory_ok = jnp.broadcast_to(usable[:, :, None], (block_count, top_count, block_len)).reshape(block_count, 1, 1, top_count * block_len)
    local_score = product('nqhd,khd->nhqk', query_heads, key_heads) * score_scale
    local_score = jnp.where(local_ok, local_score, -1e+30)
    memory_score = product('nqhd,nkhd->nhqk', query_heads, mem_key_heads) * score_scale + bias[None, :, None, None]
    memory_score = jnp.where(memory_ok, memory_score, -1e+30)
    highest = jnp.maximum(lax.optimization_barrier(jnp.max(local_score, axis=-1, keepdims=True)), lax.optimization_barrier(jnp.max(memory_score, axis=-1, keepdims=True)))
    local_exp = jnp.exp(local_score - highest)
    memory_exp = jnp.exp(memory_score - highest)
    total_mass = lax.optimization_barrier(jnp.sum(local_exp, axis=-1, keepdims=True)) + lax.optimization_barrier(jnp.sum(memory_exp, axis=-1, keepdims=True))
    local_prob = local_exp / total_mass
    memory_prob = memory_exp / total_mass
    local_weight = local_prob.astype(jnp.bfloat16)
    memory_weight = memory_prob.astype(jnp.bfloat16)
    attended = product('nhqk,khd->nqhd', local_weight, value_heads) + product('nhqk,nkhd->nqhd', memory_weight, mem_value_heads)
    local_dprob = product('nqhd,khd->nhqk', grad_heads, value_heads)
    memory_dprob = product('nqhd,nkhd->nhqk', grad_heads, mem_value_heads)
    row_delta = lax.optimization_barrier(jnp.sum(local_prob * local_dprob, axis=-1, keepdims=True)) + lax.optimization_barrier(jnp.sum(memory_prob * memory_dprob, axis=-1, keepdims=True))
    local_dscore = (local_prob * (local_dprob - row_delta) * score_scale).astype(jnp.bfloat16)
    memory_dscore = (memory_prob * (memory_dprob - row_delta) * score_scale).astype(jnp.bfloat16)
    grad_query = product('nhqk,khd->nqhd', local_dscore, key_heads) + product('nhqk,nkhd->nqhd', memory_dscore, mem_key_heads)
    local_dkey = product('nhqk,nqhd->khd', local_dscore, query_heads).reshape(seg_len, features)
    local_dvalue = product('nhqk,nqhd->khd', local_weight, grad_heads).reshape(seg_len, features)
    memory_dkey = product('nhqk,nqhd->nkhd', memory_dscore, query_heads).reshape(block_count, top_count, block_len, features)
    memory_dvalue = product('nhqk,nqhd->nkhd', memory_weight, grad_heads).reshape(block_count, top_count, block_len, features)
    return (attended.reshape(row_count, features).astype(jnp.bfloat16), grad_query.reshape(row_count, features).astype(jnp.bfloat16), local_dkey, local_dvalue, memory_dkey, memory_dvalue)

def reference(queries, keys, values, grad_out, retrieved, mem_bias):
    features = H * HD
    group_rows = min(512, TOK_DEV)
    group_blocks = group_rows // BLK
    per_segment = TOK_DEV // group_rows
    key_blocks = keys.reshape(NBLK, BLK, features)
    value_blocks = values.reshape(NBLK, BLK, features)

    def group_step(inner_carry, group_index):
        seg_kgrad, seg_vgrad, mem_kgrad, mem_vgrad = inner_carry
        segment = group_index // per_segment
        first_row = group_index % per_segment * group_rows
        row_start = group_index * group_rows
        query_rows = lax.dynamic_slice_in_dim(queries, row_start, group_rows, 0)
        grad_rows = lax.dynamic_slice_in_dim(grad_out, row_start, group_rows, 0)
        seg_keys = lax.dynamic_slice_in_dim(keys, segment * TOK_DEV, TOK_DEV, 0)
        seg_values = lax.dynamic_slice_in_dim(values, segment * TOK_DEV, TOK_DEV, 0)
        named_blocks = lax.dynamic_slice_in_dim(retrieved, group_index * group_blocks, group_blocks, 0)
        block_index = group_index * group_blocks + jnp.arange(group_blocks, dtype=jnp.int32)
        usable = named_blocks < block_index[:, None]
        flat_named = named_blocks.reshape(-1)
        mem_keys = key_blocks[flat_named].reshape(group_blocks, TOPK, BLK, features)
        mem_values = value_blocks[flat_named].reshape(group_blocks, TOPK, BLK, features)
        results = attend_group(query_rows, grad_rows, seg_keys, seg_values, mem_keys, mem_values, usable, mem_bias, first_row)
        seg_kgrad = seg_kgrad + results[2]
        seg_vgrad = seg_vgrad + results[3]
        mem_kgrad = mem_kgrad.at[flat_named].add(results[4].reshape(group_blocks * TOPK, BLK, features))
        mem_vgrad = mem_vgrad.at[flat_named].add(results[5].reshape(group_blocks * TOPK, BLK, features))
        return ((seg_kgrad, seg_vgrad, mem_kgrad, mem_vgrad), (results[0], results[1]))

    def segment_step(state_carry, segment):
        key_grad, value_grad = state_carry
        zero_seg = jnp.zeros((TOK_DEV, features), jnp.float32)
        zero_mem = jnp.zeros((NBLK, BLK, features), jnp.float32)
        groups = segment * per_segment + jnp.arange(per_segment, dtype=jnp.int32)
        inner, outputs = lax.scan(group_step, (zero_seg, zero_seg, zero_mem, zero_mem), groups)
        rounded_keys = lax.optimization_barrier(inner[2].astype(jnp.bfloat16)).astype(jnp.float32)
        rounded_values = lax.optimization_barrier(inner[3].astype(jnp.bfloat16)).astype(jnp.float32)
        key_grad = key_grad + rounded_keys
        value_grad = value_grad + rounded_values
        seg_start = segment * BLK_DEV
        local_key = lax.dynamic_slice_in_dim(key_grad, seg_start, BLK_DEV, 0) + inner[0].reshape(BLK_DEV, BLK, features)
        local_value = lax.dynamic_slice_in_dim(value_grad, seg_start, BLK_DEV, 0) + inner[1].reshape(BLK_DEV, BLK, features)
        key_grad = lax.dynamic_update_slice_in_dim(key_grad, local_key, seg_start, 0)
        value_grad = lax.dynamic_update_slice_in_dim(value_grad, local_value, seg_start, 0)
        return ((key_grad, value_grad), outputs)
    zero_grads = jnp.zeros((NBLK, BLK, features), jnp.float32)
    finals, outputs = lax.scan(segment_step, (zero_grads, zero_grads), jnp.arange(N_SEQ, dtype=jnp.int32))
    attended = outputs[0].reshape(TOKENS, features)
    grad_queries = outputs[1].reshape(TOKENS, features)
    grad_keys = finals[0].reshape(TOKENS, features).astype(jnp.bfloat16)
    grad_values = finals[1].reshape(TOKENS, features).astype(jnp.bfloat16)
    return (attended, grad_queries, grad_keys, grad_values)
```

```python
import math

import jax
import jax.numpy as jnp
from jax import lax
from jax.experimental import pallas as pl
from jax.experimental.pallas import tpu as pltpu
from jax.sharding import PartitionSpec as P

BLK = 64
NY, NX, NC = 4, 4, 2
NSEQ = NY * NX * NC
HD = 128
FEAT = 256
SEG = 512
POOL = 32
LOG2E = 1.4426950408889634
SCALE = 1.0 / math.sqrt(HD)
OFFS = (0, 1, -1, 2)
QT = 256
NSPLIT = POOL * BLK // QT


def seq_of(y, x, c):
    return (y * NX + x) * NC + c


def shift(value, dy, dx, dc):
    pairs = [
        (seq_of(y, x, c), seq_of((y + dy) % NY, (x + dx) % NX, (c + dc) % NC))
        for y in range(NY)
        for x in range(NX)
        for c in range(NC)
    ]
    return lax.ppermute(value, "seq", pairs)


def dot(a, b, dims):
    return lax.dot_general(a, b, (dims, ((), ())), preferred_element_type=jnp.float32)


NN = ((1,), (0,))
NT = ((1,), (1,))
TN = ((0,), (0,))


def iota(shape, dim):
    return lax.broadcasted_iota(jnp.int32, shape, dim)


def flag(cond):
    return jnp.where(cond, 1.0, 0.0)


def select_kernel(where_ref, tseg_ref, trow_ref, *refs):
    pieces_k, pieces_v = refs[:8], refs[8:16]
    table_ref, mask_ref = refs[16:18]
    outs_k, outs_v = refs[18:23], refs[23:28]
    prefix_ref, table_smem, table_sem, sems = refs[28:]
    me = where_ref[0]
    nid = NSEQ * 8
    ids = iota((NSEQ, nid), 1)
    flags = ids < 0
    for e in range(128):
        flags = flags | (tseg_ref[:, e : e + 1] == ids)
    wanted = flag(flags)
    row, col = iota((nid, nid), 0), iota((nid, nid), 1)
    upto = flag(row <= col)
    upto8 = flag((row <= col) & ((row >> 3) == (col >> 3)))
    prefix = dot(wanted.astype(jnp.bfloat16), upto.astype(jnp.bfloat16), NN)
    prefix8 = dot(wanted.astype(jnp.bfloat16), upto8.astype(jnp.bfloat16), NN)
    gid, gw = iota((nid, NSEQ), 0), iota((nid, NSEQ), 1)
    same = (gid >> 3) == gw
    ones = flag(same).astype(jnp.bfloat16)
    inner = jnp.where(same, (gid & 7).astype(jnp.float32), 0.0).astype(jnp.bfloat16)
    for r in range(2):
        picked = jnp.where(prefix8 == float(r + 1), wanted, 0.0)
        has = dot(picked.astype(jnp.bfloat16), ones, NN)
        block = dot(picked.astype(jnp.bfloat16), inner, NN)
        place = dot((picked * (prefix - 1.0)).astype(jnp.bfloat16), ones, NN)
        table_ref[r * NSEQ : (r + 1) * NSEQ, :] = jnp.where(has > 0.5, block, -1.0).astype(jnp.int32)
        table_ref[(2 + r) * NSEQ : (3 + r) * NSEQ, :] = place.astype(jnp.int32)
    to_smem = pltpu.make_async_copy(table_ref, table_smem, table_sem)
    to_smem.start()
    prefix_ref[...] = jnp.where(flags, prefix - 1.0, -1.0)
    mine = prefix_ref[pl.ds(me, 1), :]
    compact = flag(iota((POOL, nid), 0).astype(jnp.float32) == mine)
    named = trow_ref[pl.ds(me * 8, 8), :]
    ids8 = iota((8, nid), 1)
    used = ids8 < 0
    for e in range(16):
        used = used | (named[:, e : e + 1] == ids8)
    used = flag(used & (ids8 < me * 8 + iota((8, nid), 0)))
    spread = flag(iota((8, SEG), 0) == (iota((8, SEG), 1) >> 6))
    by_id = dot(used.astype(jnp.bfloat16), spread.astype(jnp.bfloat16), TN)
    mask_ref[...] = dot(compact.astype(jnp.bfloat16), by_id.astype(jnp.bfloat16), NN)
    to_smem.wait()
    y, x, c = me // 8, (me // 2) % 4, me % 2
    for kind, pieces, outs in ((0, pieces_k, outs_k), (1, pieces_v, outs_v)):
        for oi, off in enumerate(OFFS):
            if kind == 0:
                reader = seq_of(y, (x + off + 4) % 4, c)
            else:
                reader = seq_of((y + off + 4) % 4, x, c)
            for j in range(16):
                di, dc, r = j // 4, (j // 2) % 2, j % 2
                d = OFFS[di]
                if kind == 0:
                    writer = seq_of((y + d + 4) % 4, x, (c + dc) % 2)
                else:
                    writer = seq_of(y, (x + d + 4) % 4, (c + dc) % 2)
                block = jnp.maximum(table_smem[r * NSEQ + reader, writer], 0)
                out, at = (outs[oi], j) if oi < 3 else (outs[3 + j // 8], j % 8)
                pltpu.make_async_copy(
                    pieces[di * 2 + dc].at[pl.ds(pl.multiple_of(block * BLK, BLK), BLK), :],
                    out.at[at],
                    sems.at[kind * 5 + (oi if oi < 3 else 3 + j // 8)],
                ).start()
    for kind, outs in ((0, outs_k), (1, outs_v)):
        for i in range(5):
            pltpu.make_async_copy(outs[i], outs[i], sems.at[kind * 5 + i]).wait()


def select(where, tseg, trow, pieces_k, pieces_v):
    bf, vm, hbm = jnp.bfloat16, pltpu.VMEM, pl.ANY
    counts = (16, 16, 16, 8, 8)
    msgs = [jax.ShapeDtypeStruct((n, BLK, FEAT), bf) for n in counts] * 2
    spec = lambda space: pl.BlockSpec(memory_space=space)
    return pl.pallas_call(
        select_kernel,
        name="select",
        in_specs=[spec(pltpu.SMEM), spec(vm), spec(vm)] + [spec(hbm)] * 16,
        out_specs=[spec(vm)] * 12,
        out_shape=[
            jax.ShapeDtypeStruct((4 * NSEQ, NSEQ), jnp.int32),
            jax.ShapeDtypeStruct((POOL, SEG), jnp.float32),
        ]
        + msgs,
        scratch_shapes=[
            pltpu.VMEM((NSEQ, NSEQ * 8), jnp.float32),
            pltpu.SMEM((4 * NSEQ, NSEQ), jnp.int32),
            pltpu.SemaphoreType.DMA,
            pltpu.SemaphoreType.DMA((10,)),
        ],
        cost_estimate=pl.CostEstimate(flops=10_000_000, bytes_accessed=8 << 20, transcendentals=0),
    )(where, tseg, trow, *pieces_k, *pieces_v)


def attend_kernel(where_ref, table_ref, bias_ref, q_ref, do_ref, k_ref, v_ref, mask_ref, *refs):
    srcs = refs[:10]
    att_ref, gq_ref, dkl_ref, dvl_ref, back_ref = refs[10:15]
    kt, vt, s_ref, dp_ref, add_ref, dka, dva, dkb, dvb, sems, out_sem = refs[15:]
    me = where_ref[0]
    y, x, c = me // 8, (me // 2) % 4, me % 2
    tiles = (kt, vt)
    for kind in range(2):
        trash = jnp.int32(POOL)
        for oi, off in enumerate(OFFS):
            for j in range(16):
                di, dc, r = j // 4, (j // 2) % 2, j % 2
                d = OFFS[di]
                if kind == 0:
                    writer = seq_of((y + d + 4) % 4, (x + off + 4) % 4, (c + dc) % 2)
                else:
                    writer = seq_of((y + off + 4) % 4, (x + d + 4) % 4, (c + dc) % 2)
                has = table_ref[r * NSEQ + me, writer] >= 0
                place = jnp.where(has, table_ref[(2 + r) * NSEQ + me, writer], trash)
                trash = jnp.where(has, trash, trash + 1)
                src, at = (srcs[kind * 5 + oi], j) if oi < 3 else (srcs[kind * 5 + 3 + j // 8], j % 8)
                pltpu.make_async_copy(
                    src.at[at],
                    tiles[kind].at[pl.ds(pl.multiple_of(place * BLK, BLK), BLK), :],
                    sems.at[kind],
                ).start()
    for h in range(2):
        for i in range(NSPLIT):
            add_ref[h, i] = jnp.where(mask_ref[i * 4 : i * 4 + 4, :] > 0.5, bias_ref[h] * LOG2E, -1e30)
    for kind in range(2):
        pltpu.make_async_copy(tiles[kind], tiles[kind], sems.at[kind]).wait()

    def fold(value, op):
        return op(value.reshape(QT // 8, 8, QT), axis=0)

    for h in range(2):
        hs = slice(h * HD, (h + 1) * HD)
        for t in range(SEG // QT):
            rows = slice(t * QT, (t + 1) * QT)
            qc, doc = q_ref[rows, hs], do_ref[rows, hs]

            def mem_score(i, top):
                at = pl.ds(pl.multiple_of(i * QT, QT), QT)
                score = dot(kt[at, hs], qc, NT) * (SCALE * LOG2E)
                add = add_ref[h, i, :, rows]
                score = (score.reshape(4, BLK, QT) + add[:, None, :]).reshape(QT, QT)
                s_ref[at, :] = score
                return jnp.maximum(top, fold(score, jnp.max))

            top = jnp.full((8, QT), -1e30, jnp.float32)
            for n in range(t + 1):
                score = dot(k_ref[n * QT : (n + 1) * QT, hs], qc, NT) * (SCALE * LOG2E)
                if n == t:
                    score = jnp.where(iota((QT, QT), 0) <= iota((QT, QT), 1), score, -1e30)
                s_ref[POOL * BLK + n * QT : POOL * BLK + (n + 1) * QT, :] = score
                top = jnp.maximum(top, fold(score, jnp.max))
            top = lax.fori_loop(0, NSPLIT, mem_score, top)
            top = jnp.max(top, axis=0, keepdims=True)

            def weigh(i, mass):
                at = pl.ds(pl.multiple_of(i * QT, QT), QT)
                e = jnp.exp2(s_ref[at, :] - top)
                s_ref[at, :] = e
                return mass + fold(e, jnp.sum)

            count = NSPLIT + t + 1
            mass = lax.fori_loop(0, count, weigh, jnp.zeros((8, QT), jnp.float32))
            inv = 1.0 / jnp.sum(mass, axis=0, keepdims=True)

            def forward(at, vc, put, carry):
                out, delta = carry
                p = s_ref[at, :] * inv
                s_ref[at, :] = p
                w = p.astype(jnp.bfloat16)
                out = out + dot(vc, w, TN)
                put(dot(w, doc, NN))
                dp = dot(vc, doc, NT)
                dp_ref[at, :] = dp
                return out, delta + fold(p * dp, jnp.sum)

            def backward(at, kc, put, dq):
                ds = (s_ref[at, :] * (dp_ref[at, :] - delta) * SCALE).astype(jnp.bfloat16)
                put(dot(ds, qc, NN))
                return dq + dot(kc, ds, TN)

            def putter(ref, at):
                def put(value):
                    ref[at, hs] = value if t == 0 else ref[at, hs] + value

                return put

            def local_putter(ref, n):
                at = slice(n * QT, (n + 1) * QT)

                def put(value):
                    ref[at, hs] = value if n == t else ref[at, hs] + value

                return put

            def mem_forward(i, carry):
                at = pl.ds(pl.multiple_of(i * QT, QT), QT)
                return forward(at, vt[at, hs], putter(dva, at), carry)

            def mem_backward(i, dq):
                at = pl.ds(pl.multiple_of(i * QT, QT), QT)
                return backward(at, kt[at, hs], putter(dka, at), dq)

            carry = (jnp.zeros((HD, QT), jnp.float32), jnp.zeros((8, QT), jnp.float32))
            carry = lax.fori_loop(0, NSPLIT, mem_forward, carry)
            for n in range(t + 1):
                at = slice(POOL * BLK + n * QT, POOL * BLK + (n + 1) * QT)
                carry = forward(at, v_ref[n * QT : (n + 1) * QT, hs], local_putter(dvl_ref, n), carry)
            out, delta = carry
            delta = jnp.sum(delta, axis=0, keepdims=True)
            att_ref[rows, hs] = out.T.astype(jnp.bfloat16)
            dq = lax.fori_loop(0, NSPLIT, mem_backward, jnp.zeros((HD, QT), jnp.float32))
            for n in range(t + 1):
                at = slice(POOL * BLK + n * QT, POOL * BLK + (n + 1) * QT)
                dq = backward(at, k_ref[n * QT : (n + 1) * QT, hs], local_putter(dkl_ref, n), dq)
            gq_ref[rows, hs] = dq.T.astype(jnp.bfloat16)
    dkb[...] = dka[...].astype(jnp.bfloat16)
    dvb[...] = dva[...].astype(jnp.bfloat16)
    for w in range(NSEQ):
        for r in range(2):
            has = table_ref[r * NSEQ + me, w] >= 0
            place = jnp.where(has, table_ref[(2 + r) * NSEQ + me, w], 0)
            for kind, ref in ((0, dkb), (1, dvb)):
                pltpu.make_async_copy(
                    ref.at[pl.ds(pl.multiple_of(place * BLK, BLK), BLK), :],
                    back_ref.at[w, kind * 2 + r],
                    out_sem,
                ).start()
    pltpu.make_async_copy(back_ref, back_ref, out_sem).wait()


def attend(where, table, bias, q, do, k, v, mask, srcs):
    bf, f32, vm, hbm, sm = jnp.bfloat16, jnp.float32, pltpu.VMEM, pl.ANY, pltpu.SMEM
    spec = lambda space: pl.BlockSpec(memory_space=space)
    keys = POOL * BLK
    return pl.pallas_call(
        attend_kernel,
        name="attend",
        in_specs=[spec(sm)] * 3 + [spec(vm)] * 5 + [spec(hbm)] * 10,
        out_specs=[spec(vm)] * 4 + [spec(hbm)],
        out_shape=[
            jax.ShapeDtypeStruct((SEG, FEAT), bf),
            jax.ShapeDtypeStruct((SEG, FEAT), bf),
            jax.ShapeDtypeStruct((SEG, FEAT), f32),
            jax.ShapeDtypeStruct((SEG, FEAT), f32),
            jax.ShapeDtypeStruct((NSEQ, 4, BLK, FEAT), bf),
        ],
        scratch_shapes=[
            pltpu.VMEM((64 * BLK, FEAT), bf),
            pltpu.VMEM((64 * BLK, FEAT), bf),
            pltpu.VMEM((keys + SEG, QT), f32),
            pltpu.VMEM((keys + SEG, QT), f32),
            pltpu.VMEM((2, NSPLIT, 4, SEG), f32),
            pltpu.VMEM((keys, FEAT), f32),
            pltpu.VMEM((keys, FEAT), f32),
            pltpu.VMEM((keys, FEAT), bf),
            pltpu.VMEM((keys, FEAT), bf),
            pltpu.SemaphoreType.DMA((2,)),
            pltpu.SemaphoreType.DMA,
        ],
        cost_estimate=pl.CostEstimate(flops=8_000_000_000, bytes_accessed=16 << 20, transcendentals=3_000_000),
    )(where, table, bias, q, do, k, v, mask, *srcs)


def settle_kernel(where_ref, table_ref, dkl_ref, dvl_ref, back_ref, gk_ref, gv_ref, dk, dv):
    me = where_ref[0]
    dk[...] = dkl_ref[...]
    dv[...] = dvl_ref[...]

    def step(s, _):
        for r in range(2):
            block = table_ref[r * NSEQ + s, me]

            @pl.when(block >= 0)
            def _():
                at = pl.ds(pl.multiple_of(block * BLK, BLK), BLK)
                dk[at, :] += back_ref[s, r].astype(jnp.float32)
                dv[at, :] += back_ref[s, 2 + r].astype(jnp.float32)

        return 0

    lax.fori_loop(0, NSEQ, step, 0)
    gk_ref[...] = dk[...].astype(jnp.bfloat16)
    gv_ref[...] = dv[...].astype(jnp.bfloat16)


def settle(where, table, dkl, dvl, back):
    spec = lambda space: pl.BlockSpec(memory_space=space)
    return pl.pallas_call(
        settle_kernel,
        name="settle",
        in_specs=[spec(pltpu.SMEM)] * 2 + [spec(pltpu.VMEM)] * 3,
        out_specs=[spec(pltpu.VMEM)] * 2,
        out_shape=[jax.ShapeDtypeStruct((SEG, FEAT), jnp.bfloat16)] * 2,
        scratch_shapes=[pltpu.VMEM((SEG, FEAT), jnp.float32)] * 2,
        cost_estimate=pl.CostEstimate(flops=2_000_000, bytes_accessed=6 << 20, transcendentals=0),
    )(where, table, dkl, dvl, back)


def shards(queries, keys, values, grad_out, retrieved, mem_bias):
    where = lax.axis_index("seq").astype(jnp.int32).reshape(1)
    devices = lax.axis_size("seq") * lax.axis_size("head")
    copies = jnp.broadcast_to(retrieved, (devices, *retrieved.shape))
    lists = lax.all_to_all(copies, ("seq", "head"), split_axis=0, concat_axis=0, tiled=True)
    trow = lists.reshape(devices, 16)
    tseg = lists.reshape(NSEQ, 128)
    col_k = [keys] + [shift(keys, -d, 0, 0) for d in OFFS[1:]]
    row_v = [values] + [shift(values, 0, -d, 0) for d in OFFS[1:]]
    pieces_k = [p for piece in col_k for p in (piece, shift(piece, 0, 0, 1))]
    pieces_v = [p for piece in row_v for p in (piece, shift(piece, 0, 0, 1))]
    table, mask, *msgs = select(where, tseg, trow, pieces_k, pieces_v)
    k0, kp, km, ka, kb, v0, vp, vm, va, vb = msgs
    ka = shift(ka, 0, 1, 0)
    va = shift(va, 1, 0, 0)
    kb = shift(kb, 0, -1, 0)
    vb = shift(vb, -1, 0, 0)
    srcs = [
        k0,
        shift(km, 0, -1, 0),
        shift(kp, 0, 1, 0),
        shift(ka, 0, 1, 0),
        shift(kb, 0, -1, 0),
        v0,
        shift(vm, -1, 0, 0),
        shift(vp, 1, 0, 0),
        shift(va, 1, 0, 0),
        shift(vb, -1, 0, 0),
    ]
    attended, grad_queries, dkl, dvl, back = attend(
        where, table, mem_bias, queries, grad_out, keys, values, mask, srcs
    )
    back = lax.all_to_all(back, "seq", split_axis=0, concat_axis=0, tiled=True)
    grad_keys, grad_values = settle(where, table, dkl, dvl, back)
    return attended, grad_queries, grad_keys, grad_values


def solution(mesh):
    whole = P("seq", "head")
    return jax.shard_map(
        shards,
        mesh=mesh,
        in_specs=(whole, whole, whole, whole, P(("seq", "head"), None), P("head")),
        out_specs=(whole, whole, whole, whole),
        check_vma=False,
    )
```

```python
import math

import jax
import jax.numpy as jnp
from jax import lax
from jax.experimental import pallas as pl
from jax.experimental.pallas import tpu as pltpu
from jax.sharding import PartitionSpec as P


BLK = 64
NY, NX, NC = 4, 4, 2
NSEQ = NY * NX * NC
HD = 128
FEAT = 256
SEG = 512
POOL = 32
LOG2E = 1.4426950408889634
SCALE = 1.0 / math.sqrt(HD)
OFFS = (0, 1, -1, 2)
QT = 256
KC = 256
NSPLIT = POOL * BLK // KC
SPC = KC // BLK


def seq_of(y, x, c):
    return (y * NX + x) * NC + c


def shift(value, dy, dx, dc):
    pairs = [
        (seq_of(y, x, c), seq_of((y + dy) % NY, (x + dx) % NX, (c + dc) % NC))
        for y in range(NY)
        for x in range(NX)
        for c in range(NC)
    ]
    return lax.ppermute(value, "seq", pairs)


def dot(a, b, dims):
    return lax.dot_general(a, b, (dims, ((), ())), preferred_element_type=jnp.float32)


NN = ((1,), (0,))
NT = ((1,), (1,))
TN = ((0,), (0,))


def iota(shape, dim):
    return lax.broadcasted_iota(jnp.int32, shape, dim)


def flag(cond):
    return jnp.where(cond, 1.0, 0.0)


def select_kernel(where_ref, tseg_ref, trow_ref, *refs):
    pieces_k, pieces_v = refs[:8], refs[8:16]
    table_ref, mask_ref = refs[16:18]
    outs = refs[18:30]
    prefix_ref, table_smem, table_sem, sems = refs[30:]
    me = where_ref[0]
    nid = NSEQ * 8
    ids = iota((NSEQ, nid), 1)
    flags = ids < 0
    for e in range(128):
        flags = flags | (tseg_ref[:, e : e + 1] == ids)
    wanted = flag(flags)
    row, col = iota((nid, nid), 0), iota((nid, nid), 1)
    upto = flag(row <= col)
    upto8 = flag((row <= col) & ((row >> 3) == (col >> 3)))
    prefix = dot(wanted.astype(jnp.bfloat16), upto.astype(jnp.bfloat16), NN)
    prefix8 = dot(wanted.astype(jnp.bfloat16), upto8.astype(jnp.bfloat16), NN)
    gid, gw = iota((nid, NSEQ), 0), iota((nid, NSEQ), 1)
    same = (gid >> 3) == gw
    ones = flag(same).astype(jnp.bfloat16)
    inner = jnp.where(same, (gid & 7).astype(jnp.float32), 0.0).astype(jnp.bfloat16)
    for r in range(2):
        picked = jnp.where(prefix8 == float(r + 1), wanted, 0.0)
        has = dot(picked.astype(jnp.bfloat16), ones, NN)
        block = dot(picked.astype(jnp.bfloat16), inner, NN)
        place = dot((picked * (prefix - 1.0)).astype(jnp.bfloat16), ones, NN)
        table_ref[r * NSEQ : (r + 1) * NSEQ, :] = jnp.where(has > 0.5, block, -1.0).astype(jnp.int32)
        spare = iota((NSEQ, NSEQ), 1) + POOL + NSEQ * r
        table_ref[(2 + r) * NSEQ : (3 + r) * NSEQ, :] = jnp.where(has > 0.5, place.astype(jnp.int32), spare)
    to_smem = pltpu.make_async_copy(table_ref, table_smem, table_sem)
    to_smem.start()
    prefix_ref[...] = jnp.where(flags, prefix - 1.0, -1.0)
    mine = prefix_ref[pl.ds(me, 1), :]
    compact = flag(iota((POOL, nid), 0).astype(jnp.float32) == mine)
    named = trow_ref[pl.ds(me * 8, 8), :]
    ids8 = iota((8, nid), 1)
    used = ids8 < 0
    for e in range(16):
        used = used | (named[:, e : e + 1] == ids8)
    used = flag(used & (ids8 < me * 8 + iota((8, nid), 0)))
    spread = flag(iota((8, SEG), 0) == (iota((8, SEG), 1) >> 6))
    by_id = dot(used.astype(jnp.bfloat16), spread.astype(jnp.bfloat16), TN)
    mask_ref[...] = dot(compact.astype(jnp.bfloat16), by_id.astype(jnp.bfloat16), NN)
    to_smem.wait()
    y, x, c = me // 8, (me // 2) % 4, me % 2
    for kind, pieces in ((0, pieces_k), (1, pieces_v)):
        for oi, off in enumerate(OFFS[1:]):
            if kind == 0:
                reader = seq_of(y, (x + off + 4) % 4, c)
            else:
                reader = seq_of((y + off + 4) % 4, x, c)
            for j in range(16):
                di, dc, r = j // 4, (j // 2) % 2, j % 2
                d = OFFS[di]
                if kind == 0:
                    writer = seq_of((y + d + 4) % 4, x, (c + dc) % 2)
                else:
                    writer = seq_of(y, (x + d + 4) % 4, (c + dc) % 2)
                block = jnp.maximum(table_smem[r * NSEQ + reader, writer], 0)
                rows = pl.ds(pl.multiple_of(block * BLK, BLK), BLK)
                for h in range(2):
                    i = h * 6 + kind * 3 + oi
                    pltpu.make_async_copy(
                        pieces[di * 2 + dc].at[rows, pl.ds(h * HD, HD)], outs[i].at[j], sems.at[i]
                    ).start()
    for i in range(12):
        pltpu.make_async_copy(outs[i], outs[i], sems.at[i]).wait()


def select(where, tseg, trow, pieces_k, pieces_v):
    spec = lambda space: pl.BlockSpec(memory_space=space)
    return pl.pallas_call(
        select_kernel,
        name="select",
        in_specs=[spec(pltpu.SMEM), spec(pltpu.VMEM), spec(pltpu.VMEM)] + [spec(pl.ANY)] * 16,
        out_specs=[spec(pltpu.VMEM)] * 14,
        out_shape=[
            jax.ShapeDtypeStruct((4 * NSEQ, NSEQ), jnp.int32),
            jax.ShapeDtypeStruct((POOL, SEG), jnp.float32),
        ]
        + [jax.ShapeDtypeStruct((16, BLK, HD), jnp.bfloat16)] * 12,
        scratch_shapes=[
            pltpu.VMEM((NSEQ, NSEQ * 8), jnp.float32),
            pltpu.SMEM((4 * NSEQ, NSEQ), jnp.int32),
            pltpu.SemaphoreType.DMA,
            pltpu.SemaphoreType.DMA((12,)),
        ],
        cost_estimate=pl.CostEstimate(flops=10_000_000, bytes_accessed=8 << 20, transcendentals=0),
    )(where, tseg, trow, *pieces_k, *pieces_v)


def attend_kernel(h, where_ref, table_ref, bias_ref, q_ref, do_ref, k_ref, v_ref, mask_ref, *refs):
    pieces = (refs[:8], refs[8:16])
    srcs = (refs[16:19], refs[19:22])
    refs = refs[22 + 2 * h :]
    att_hbm, gq_hbm, dkl_ref, dvl_ref, back_ref = refs[:5]
    kt, vt, s_ref, dp_ref, add_ref, dka, dva, dkb, dvb, att_ref, gq_ref, sems, out_sem, end_sem = refs[5:]
    me = where_ref[0]
    y, x, c = me // 8, (me // 2) % 4, me % 2
    tiles = (kt, vt)
    hs = slice(h * HD, (h + 1) * HD)
    for kind in range(2):
        for oi, off in enumerate(OFFS):
            for j in range(16):
                di, dc, r = j // 4, (j // 2) % 2, j % 2
                d = OFFS[di]
                if kind == 0:
                    writer = seq_of((y + d + 4) % 4, (x + off + 4) % 4, (c + dc) % 2)
                else:
                    writer = seq_of((y + off + 4) % 4, (x + d + 4) % 4, (c + dc) % 2)
                place = table_ref[(2 + r) * NSEQ + me, writer]
                if oi == 0:
                    block = jnp.maximum(table_ref[r * NSEQ + me, writer], 0)
                    rows = pl.ds(pl.multiple_of(block * BLK, BLK), BLK)
                    src = pieces[kind][di * 2 + dc].at[rows, pl.ds(h * HD, HD)]
                else:
                    src = srcs[kind][oi - 1].at[j]
                pltpu.make_async_copy(
                    src,
                    tiles[kind].at[pl.ds(pl.multiple_of(place * BLK, BLK), BLK), :],
                    sems.at[kind],
                ).start()
    for i in range(NSPLIT):
        add_ref[i] = jnp.where(mask_ref[i * SPC : (i + 1) * SPC, :] > 0.5, bias_ref[h] * LOG2E, -1e30)
    keys = POOL * BLK

    def fold(value, op):
        return op(value.reshape(KC // 8, 8, QT), axis=0)

    for kind in range(2):
        all_slots = tiles[kind].at[pl.ds(0, 2 * NSEQ * BLK), :]
        pltpu.make_async_copy(all_slots, all_slots, sems.at[kind]).wait()

    for t in range(SEG // QT):
        rows = slice(t * QT, (t + 1) * QT)
        qc, doc = q_ref[rows, hs], do_ref[rows, hs]
        local = (t + 1) * QT // KC

        def mem_score(i, top):
            at = pl.ds(pl.multiple_of(i * KC, KC), KC)
            score = dot(kt[at, :], qc, NT) * (SCALE * LOG2E)
            add = add_ref[i, :, rows]
            score = (score.reshape(SPC, BLK, QT) + add[:, None, :]).reshape(KC, QT)
            s_ref[at, :] = score
            return jnp.maximum(top, fold(score, jnp.max))

        top = jnp.full((8, QT), -1e30, jnp.float32)
        for n in range(local):
            score = dot(k_ref[n * KC : (n + 1) * KC, hs], qc, NT) * (SCALE * LOG2E)
            if (n + 1) * KC > t * QT:
                score = jnp.where(iota((KC, QT), 0) + n * KC <= iota((KC, QT), 1) + t * QT, score, -1e30)
            s_ref[keys + n * KC : keys + (n + 1) * KC, :] = score
            top = jnp.maximum(top, fold(score, jnp.max))
        top = lax.fori_loop(0, NSPLIT, mem_score, top)
        top = jnp.max(top, axis=0, keepdims=True)

        def weigh(i, mass):
            at = pl.ds(pl.multiple_of(i * KC, KC), KC)
            e = jnp.exp2(s_ref[at, :] - top)
            s_ref[at, :] = e
            return mass + fold(e, jnp.sum)

        mass = lax.fori_loop(0, NSPLIT + local, weigh, jnp.zeros((8, QT), jnp.float32))
        inv = 1.0 / jnp.sum(mass, axis=0, keepdims=True)

        def forward(at, vc, put, carry):
            out, delta = carry
            p = s_ref[at, :] * inv
            s_ref[at, :] = p
            w = p.astype(jnp.bfloat16)
            out = out + dot(vc, w, TN)
            put(dot(w, doc, NN))
            dp = dot(vc, doc, NT)
            dp_ref[at, :] = dp
            return out, delta + fold(p * dp, jnp.sum)

        def backward(at, kc, put, dq):
            ds = (s_ref[at, :] * (dp_ref[at, :] - delta) * SCALE).astype(jnp.bfloat16)
            put(dot(ds, qc, NN))
            return dq + dot(kc, ds, TN)

        def putter(ref, at):
            def put(value):
                ref[at, :] = value if t == 0 else ref[at, :] + value

            return put

        def local_putter(ref, n):
            at = slice(n * KC, (n + 1) * KC)

            def put(value):
                ref[at, :] = value if n * KC >= t * QT else ref[at, :] + value

            return put

        def mem_forward(i, carry):
            at = pl.ds(pl.multiple_of(i * KC, KC), KC)
            return forward(at, vt[at, :], putter(dva, at), carry)

        def mem_backward(i, dq):
            at = pl.ds(pl.multiple_of(i * KC, KC), KC)
            return backward(at, kt[at, :], putter(dka, at), dq)

        carry = (jnp.zeros((HD, QT), jnp.float32), jnp.zeros((8, QT), jnp.float32))
        carry = lax.fori_loop(0, NSPLIT, mem_forward, carry)
        for n in range(local):
            at = slice(keys + n * KC, keys + (n + 1) * KC)
            carry = forward(at, v_ref[n * KC : (n + 1) * KC, hs], local_putter(dvl_ref, n), carry)
        out, delta = carry
        delta = jnp.sum(delta, axis=0, keepdims=True)
        att_ref[rows, :] = out.T.astype(jnp.bfloat16)
        dq = lax.fori_loop(0, NSPLIT, mem_backward, jnp.zeros((HD, QT), jnp.float32))
        for n in range(local):
            at = slice(keys + n * KC, keys + (n + 1) * KC)
            dq = backward(at, k_ref[n * KC : (n + 1) * KC, hs], local_putter(dkl_ref, n), dq)
        gq_ref[rows, :] = dq.T.astype(jnp.bfloat16)
    ends = [
        pltpu.make_async_copy(src, dst.at[:, pl.ds(h * HD, HD)], end_sem.at[i])
        for i, (src, dst) in enumerate(((att_ref, att_hbm), (gq_ref, gq_hbm)))
    ]
    for copy in ends:
        copy.start()
    dkb[...] = dka[...].astype(jnp.bfloat16)
    dvb[...] = dva[...].astype(jnp.bfloat16)
    for w in range(NSEQ):
        for r in range(2):
            place = jnp.minimum(table_ref[(2 + r) * NSEQ + me, w], POOL - 1)
            for kind, ref in ((0, dkb), (1, dvb)):
                pltpu.make_async_copy(
                    ref.at[pl.ds(pl.multiple_of(place * BLK, BLK), BLK), :],
                    back_ref.at[w, kind * 2 + r],
                    out_sem,
                ).start()
    pltpu.make_async_copy(back_ref, back_ref, out_sem).wait()
    for copy in ends:
        copy.wait()


def attend(h, where, table, bias, q, do, k, v, mask, pieces_k, pieces_v, srcs, done):
    bf, f32, vm, hbm, sm = jnp.bfloat16, jnp.float32, pltpu.VMEM, pl.ANY, pltpu.SMEM
    spec = lambda space: pl.BlockSpec(memory_space=space)
    keys = POOL * BLK
    extra = list(done)
    return pl.pallas_call(
        lambda *refs: attend_kernel(h, *refs),
        in_specs=[spec(sm)] * 3 + [spec(vm)] * 5 + [spec(hbm)] * (22 + len(extra)),
        out_specs=[spec(hbm)] * 2 + [spec(vm)] * 2 + [spec(hbm)],
        out_shape=[
            jax.ShapeDtypeStruct((SEG, FEAT), bf),
            jax.ShapeDtypeStruct((SEG, FEAT), bf),
            jax.ShapeDtypeStruct((SEG, HD), f32),
            jax.ShapeDtypeStruct((SEG, HD), f32),
            jax.ShapeDtypeStruct((NSEQ, 4, BLK, HD), bf),
        ],
        scratch_shapes=[
            pltpu.VMEM((96 * BLK, HD), bf),
            pltpu.VMEM((96 * BLK, HD), bf),
            pltpu.VMEM((keys + SEG, QT), f32),
            pltpu.VMEM((keys + SEG, QT), f32),
            pltpu.VMEM((NSPLIT, SPC, SEG), f32),
            pltpu.VMEM((keys, HD), f32),
            pltpu.VMEM((keys, HD), f32),
            pltpu.VMEM((keys, HD), bf),
            pltpu.VMEM((keys, HD), bf),
            pltpu.VMEM((SEG, HD), bf),
            pltpu.VMEM((SEG, HD), bf),
            pltpu.SemaphoreType.DMA((2,)),
            pltpu.SemaphoreType.DMA,
            pltpu.SemaphoreType.DMA((2,)),
        ],
        input_output_aliases={30: 0, 31: 1} if extra else {},
        cost_estimate=pl.CostEstimate(flops=16_000_000_000, bytes_accessed=8 << 20, transcendentals=1_500_000),
    )(where, table, bias, q, do, k, v, mask, *pieces_k, *pieces_v, *srcs, *extra)


def settle_kernel(h, where_ref, table_ref, dkl_ref, dvl_ref, back_ref, *refs):
    gk_hbm, gv_hbm, dk, dv, dkb, dvb, sems = refs[2 * h :]
    me = where_ref[0]
    dk[...] = dkl_ref[...]
    dv[...] = dvl_ref[...]

    def step(s, _):
        for r in range(2):
            block = table_ref[r * NSEQ + s, me]

            @pl.when(block >= 0)
            def _():
                at = pl.ds(pl.multiple_of(block * BLK, BLK), BLK)
                dk[at, :] += back_ref[s, r].astype(jnp.float32)
                dv[at, :] += back_ref[s, 2 + r].astype(jnp.float32)

        return 0

    lax.fori_loop(0, NSEQ, step, 0)
    dkb[...] = dk[...].astype(jnp.bfloat16)
    dvb[...] = dv[...].astype(jnp.bfloat16)
    ends = [
        pltpu.make_async_copy(src, dst.at[:, pl.ds(h * HD, HD)], sems.at[i])
        for i, (src, dst) in enumerate(((dkb, gk_hbm), (dvb, gv_hbm)))
    ]
    for copy in ends:
        copy.start()
    for copy in ends:
        copy.wait()


def settle(h, where, table, dkl, dvl, back, done):
    spec = lambda space: pl.BlockSpec(memory_space=space)
    extra = list(done)
    return pl.pallas_call(
        lambda *refs: settle_kernel(h, *refs),
        in_specs=[spec(pltpu.SMEM)] * 2 + [spec(pltpu.VMEM)] * 3 + [spec(pl.ANY)] * len(extra),
        out_specs=[spec(pl.ANY)] * 2,
        out_shape=[jax.ShapeDtypeStruct((SEG, FEAT), jnp.bfloat16)] * 2,
        scratch_shapes=[pltpu.VMEM((SEG, HD), jnp.float32)] * 2
        + [pltpu.VMEM((SEG, HD), jnp.bfloat16)] * 2
        + [pltpu.SemaphoreType.DMA((2,))],
        input_output_aliases={5: 0, 6: 1} if extra else {},
        cost_estimate=pl.CostEstimate(flops=2_000_000, bytes_accessed=3 << 20, transcendentals=0),
    )(where, table, dkl, dvl, back, *extra)


def layer(queries, keys, values, grad_out, retrieved, mem_bias):
    where = lax.axis_index("seq").astype(jnp.int32).reshape(1)
    devices = lax.axis_size("seq") * lax.axis_size("head")
    copies = jnp.broadcast_to(retrieved, (devices, *retrieved.shape))
    lists = lax.all_to_all(copies, ("seq", "head"), split_axis=0, concat_axis=0, tiled=True)
    trow = lists.reshape(devices, 16)
    tseg = lists.reshape(NSEQ, 128)
    col_k = [keys] + [shift(keys, -d, 0, 0) for d in OFFS[1:]]
    row_v = [values] + [shift(values, 0, -d, 0) for d in OFFS[1:]]
    pieces_k = [p for piece in col_k for p in (piece, shift(piece, 0, 0, 1))]
    pieces_v = [p for piece in row_v for p in (piece, shift(piece, 0, 0, 1))]
    table, mask, *msgs = select(where, tseg, trow, pieces_k, pieces_v)
    near_k, near_v = shift(msgs[8], 0, -1, 0), shift(msgs[11], -1, 0, 0)
    fetched = []
    for h in range(2):
        kp, km, k2, vp, vm, v2 = msgs[h * 6 : h * 6 + 6]
        if h == 0:
            far_k, far_v = shift(k2, 0, 2, 0), shift(v2, 2, 0, 0)
        else:
            far_k, far_v = shift(near_k, 0, -1, 0), shift(near_v, -1, 0, 0)
        fetched.append(
            [
                shift(km, 0, -1, 0),
                shift(kp, 0, 1, 0),
                far_k,
                shift(vm, -1, 0, 0),
                shift(vp, 1, 0, 0),
                far_v,
            ]
        )
    rows, grads = (), ()
    parts = []
    for h in range(2):
        *rows, dkl, dvl, back = attend(
            h, where, table, mem_bias, queries, grad_out, keys, values, mask, pieces_k, pieces_v, fetched[h], rows
        )
        back = lax.all_to_all(back, "seq", split_axis=0, concat_axis=0, tiled=True)
        parts.append((dkl, dvl, back))
    for h in range(2):
        grads = settle(h, where, table, *parts[h], grads)
    return *rows, *grads


def solution(mesh):
    whole = P("seq", "head")
    return jax.shard_map(
        layer,
        mesh=mesh,
        in_specs=(whole, whole, whole, whole, P(("seq", "head"), None), P("head")),
        out_specs=(whole, whole, whole, whole),
        check_vma=False,
    )
```

```python
import math

import jax
import jax.numpy as jnp
from jax import lax
from jax.experimental import pallas as pl
from jax.experimental.pallas import tpu as pltpu
from jax.sharding import PartitionSpec as P


BLK = 64
NY, NX, NC = 4, 4, 2
NSEQ = NY * NX * NC
HD = 128
FEAT = 256
SEG = 512
POOL = 32
LOG2E = 1.4426950408889634
SCALE = 1.0 / math.sqrt(HD)
OFFS = (0, 1, -1, 2)
QT = 512
KC = 256
NSPLIT = POOL * BLK // KC
SPC = KC // BLK


def seq_of(y, x, c):
    return (y * NX + x) * NC + c


def shift(value, dy, dx, dc):
    pairs = [
        (seq_of(y, x, c), seq_of((y + dy) % NY, (x + dx) % NX, (c + dc) % NC))
        for y in range(NY)
        for x in range(NX)
        for c in range(NC)
    ]
    return lax.ppermute(value, "seq", pairs)


def dot(a, b, dims):
    return lax.dot_general(a, b, (dims, ((), ())), preferred_element_type=jnp.float32)


NN = ((1,), (0,))
NT = ((1,), (1,))
TN = ((0,), (0,))


def iota(shape, dim):
    return lax.broadcasted_iota(jnp.int32, shape, dim)


def flag(cond):
    return jnp.where(cond, 1.0, 0.0)


def order_of(me, y, x, c):
    return ((c ^ (me % 2)) * NY + (y ^ (me // 8))) * NX + (x ^ ((me // 2) % 4))


def prep_kernel(where_ref, lists_ref, table_ref, mask_ref):
    me, head = where_ref[0], where_ref[1]
    nid = NSEQ * 8
    ids = iota((NSEQ, nid), 1)
    flags = ids < 0
    for e in range(128):
        flags = flags | (lists_ref[:, e : e + 1] == ids)
    wanted = flag(flags)
    row, col = iota((nid, nid), 0), iota((nid, nid), 1)
    upto = flag(row <= col)
    upto8 = flag((row <= col) & ((row >> 3) == (col >> 3)))
    prefix = dot(wanted.astype(jnp.bfloat16), upto.astype(jnp.bfloat16), NN)
    prefix8 = dot(wanted.astype(jnp.bfloat16), upto8.astype(jnp.bfloat16), NN)
    gid, gw = iota((nid, NSEQ), 0), iota((nid, NSEQ), 1)
    same = (gid >> 3) == gw
    ones = flag(same).astype(jnp.bfloat16)
    inner = jnp.where(same, (gid & 7).astype(jnp.float32), 0.0).astype(jnp.bfloat16)
    for r in range(2):
        picked = jnp.where(prefix8 == float(r + 1), wanted, 0.0)
        has = dot(picked.astype(jnp.bfloat16), ones, NN)
        block = dot(picked.astype(jnp.bfloat16), inner, NN)
        place = dot((picked * (prefix - 1.0)).astype(jnp.bfloat16), ones, NN)
        table_ref[r * NSEQ : (r + 1) * NSEQ, :] = jnp.where(has > 0.5, block, -1.0).astype(jnp.int32)
        spare = iota((NSEQ, NSEQ), 1) + POOL + NSEQ * r
        table_ref[(2 + r) * NSEQ : (3 + r) * NSEQ, :] = jnp.where(has > 0.5, place.astype(jnp.int32), spare)
    mine = jnp.where(flags, prefix - 1.0, -1.0)[0:1, :]
    compact = flag(iota((POOL, nid), 0).astype(jnp.float32) == mine)
    own = lists_ref[0:1, :]
    ids8, row8 = iota((8, nid), 1), iota((8, nid), 0)
    used = ids8 < 0
    for e in range(16):
        named = jnp.zeros((8, nid), jnp.int32)
        for j in range(8):
            named = jnp.where(row8 == j, own[:, j * 16 + e : j * 16 + e + 1], named)
        used = used | (named == ids8)
    used = flag(used & (ids8 < me * 8 + (row8 ^ head)))
    spread = flag((iota((8, SEG), 0) ^ head) == (iota((8, SEG), 1) >> 6))
    by_id = dot(used.astype(jnp.bfloat16), spread.astype(jnp.bfloat16), TN)
    mask_ref[...] = dot(compact.astype(jnp.bfloat16), by_id.astype(jnp.bfloat16), NN)


def prep(where, lists):
    return pl.pallas_call(
        prep_kernel,
        name="prep",
        in_specs=[pl.BlockSpec(memory_space=pltpu.SMEM), pl.BlockSpec(memory_space=pltpu.VMEM)],
        out_specs=[pl.BlockSpec(memory_space=pltpu.VMEM)] * 2,
        out_shape=[
            jax.ShapeDtypeStruct((4 * NSEQ, NSEQ), jnp.int32),
            jax.ShapeDtypeStruct((POOL, SEG), jnp.float32),
        ],
        cost_estimate=pl.CostEstimate(flops=10_000_000, bytes_accessed=1 << 20, transcendentals=0),
    )(where, lists)


def select_kernel(where_ref, table_ref, *refs):
    pieces_k, pieces_v = refs[:8], refs[8:16]
    outs, sems = refs[16:28], refs[28]
    me = where_ref[0]
    y, x, c = me // 8, (me // 2) % 4, me % 2
    for oi, off in enumerate(OFFS[1:]):
        for kind, pieces in ((0, pieces_k), (1, pieces_v)):
            if kind == 0:
                reader = order_of(me, y, (x + off + 4) % 4, c)
            else:
                reader = order_of(me, (y + off + 4) % 4, x, c)
            for j in range(16):
                di, dc, r = j // 4, (j // 2) % 2, j % 2
                d = OFFS[di]
                if kind == 0:
                    writer = seq_of((y + d + 4) % 4, x, (c + dc) % 2)
                else:
                    writer = seq_of(y, (x + d + 4) % 4, (c + dc) % 2)
                block = jnp.maximum(table_ref[r * NSEQ + reader, writer], 0)
                rows = pl.ds(pl.multiple_of(block * BLK, BLK), BLK)
                for h in range(2):
                    i = h * 6 + kind * 3 + oi
                    pltpu.make_async_copy(
                        pieces[di * 2 + dc].at[rows, pl.ds(h * HD, HD)], outs[i].at[j], sems.at[i]
                    ).start()
    for i in range(12):
        pltpu.make_async_copy(outs[i], outs[i], sems.at[i]).wait()


def select(where, table, pieces_k, pieces_v):
    spec = lambda space: pl.BlockSpec(memory_space=space)
    return pl.pallas_call(
        select_kernel,
        name="select",
        in_specs=[spec(pltpu.SMEM)] * 2 + [spec(pl.ANY)] * 16,
        out_specs=[spec(pltpu.VMEM)] * 12,
        out_shape=[jax.ShapeDtypeStruct((16, BLK, HD), jnp.bfloat16)] * 12,
        scratch_shapes=[pltpu.SemaphoreType.DMA((12,))],
        cost_estimate=pl.CostEstimate(flops=1_000_000, bytes_accessed=6 << 20, transcendentals=0),
    )(where, table, *pieces_k, *pieces_v)


def attend_kernel(h, where_ref, table_ref, bias_ref, q_ref, do_ref, k_ref, v_ref, mask_ref, *refs):
    pieces = (refs[:8], refs[8:16])
    srcs = (refs[16:19], refs[19:22])
    refs = refs[22 + 2 * h :]
    att_hbm, gq_hbm, dkl_ref, dvl_ref, back_ref = refs[:5]
    kt, vt, s_ref, dp_ref, add_ref, dka, dva, dkb, dvb, att_ref, gq_ref, sems, out_sem, end_sem = refs[5:]
    me = where_ref[0]
    y, x, c = me // 8, (me // 2) % 4, me % 2
    tiles = (kt, vt)
    hs = slice(h * HD, (h + 1) * HD)
    for kind in range(2):
        for oi, off in enumerate(OFFS):
            for j in range(16):
                di, dc, r = j // 4, (j // 2) % 2, j % 2
                d = OFFS[di]
                if kind == 0:
                    writer = seq_of((y + d + 4) % 4, (x + off + 4) % 4, (c + dc) % 2)
                else:
                    writer = seq_of((y + off + 4) % 4, (x + d + 4) % 4, (c + dc) % 2)
                place = table_ref[(2 + r) * NSEQ, writer]
                if oi == 0:
                    block = jnp.maximum(table_ref[r * NSEQ, writer], 0)
                    rows = pl.ds(pl.multiple_of(block * BLK, BLK), BLK)
                    src = pieces[kind][di * 2 + dc].at[rows, pl.ds(h * HD, HD)]
                else:
                    src = srcs[kind][oi - 1].at[j]
                pltpu.make_async_copy(
                    src,
                    tiles[kind].at[pl.ds(pl.multiple_of(place * BLK, BLK), BLK), :],
                    sems.at[kind],
                ).start()
    for i in range(NSPLIT):
        add_ref[i] = jnp.where(mask_ref[i * SPC : (i + 1) * SPC, :] > 0.5, bias_ref[h] * LOG2E, -1e30)
    keys = POOL * BLK

    def fold(value, op):
        return op(value.reshape(KC // 8, 8, QT), axis=0)

    for kind in range(2):
        all_slots = tiles[kind].at[pl.ds(0, 2 * NSEQ * BLK), :]
        pltpu.make_async_copy(all_slots, all_slots, sems.at[kind]).wait()

    for t in range(SEG // QT):
        rows = slice(t * QT, (t + 1) * QT)
        qc, doc = q_ref[rows, hs], do_ref[rows, hs]
        local = (t + 1) * QT // KC

        def mem_score(i, top):
            at = pl.ds(pl.multiple_of(i * KC, KC), KC)
            score = dot(kt[at, :], qc, NT) * (SCALE * LOG2E)
            add = add_ref[i, :, rows]
            score = (score.reshape(SPC, BLK, QT) + add[:, None, :]).reshape(KC, QT)
            s_ref[at, :] = score
            return jnp.maximum(top, fold(score, jnp.max))

        top = jnp.full((8, QT), -1e30, jnp.float32)
        for n in range(local):
            score = dot(k_ref[n * KC : (n + 1) * KC, hs], qc, NT) * (SCALE * LOG2E)
            if (n + 1) * KC > t * QT:
                score = jnp.where(iota((KC, QT), 0) + n * KC <= iota((KC, QT), 1) + t * QT, score, -1e30)
            s_ref[keys + n * KC : keys + (n + 1) * KC, :] = score
            top = jnp.maximum(top, fold(score, jnp.max))
        top = lax.fori_loop(0, NSPLIT, mem_score, top)
        top = jnp.max(top, axis=0, keepdims=True)

        def weigh(i, mass):
            at = pl.ds(pl.multiple_of(i * KC, KC), KC)
            e = jnp.exp2(s_ref[at, :] - top)
            s_ref[at, :] = e
            return mass + fold(e, jnp.sum)

        mass = lax.fori_loop(0, NSPLIT + local, weigh, jnp.zeros((8, QT), jnp.float32))
        inv = 1.0 / jnp.sum(mass, axis=0, keepdims=True)

        def forward(at, vc, put, carry):
            out, delta = carry
            p = s_ref[at, :] * inv
            s_ref[at, :] = p
            w = p.astype(jnp.bfloat16)
            out = out + dot(vc, w, TN)
            put(dot(w, doc, NN))
            dp = dot(vc, doc, NT)
            dp_ref[at, :] = dp
            return out, delta + fold(p * dp, jnp.sum)

        def backward(at, kc, put, dq):
            ds = (s_ref[at, :] * (dp_ref[at, :] - delta) * SCALE).astype(jnp.bfloat16)
            put(dot(ds, qc, NN))
            return dq + dot(kc, ds, TN)

        def putter(ref, at):
            def put(value):
                ref[at, :] = value if t == 0 else ref[at, :] + value

            return put

        def local_putter(ref, n):
            at = slice(n * KC, (n + 1) * KC)

            def put(value):
                ref[at, :] = value if n * KC >= t * QT else ref[at, :] + value

            return put

        def mem_forward(i, carry):
            at = pl.ds(pl.multiple_of(i * KC, KC), KC)
            return forward(at, vt[at, :], putter(dva, at), carry)

        def mem_backward(i, dq):
            at = pl.ds(pl.multiple_of(i * KC, KC), KC)
            return backward(at, kt[at, :], putter(dka, at), dq)

        carry = (jnp.zeros((HD, QT), jnp.float32), jnp.zeros((8, QT), jnp.float32))
        carry = lax.fori_loop(0, NSPLIT, mem_forward, carry)
        for n in range(local):
            at = slice(keys + n * KC, keys + (n + 1) * KC)
            carry = forward(at, v_ref[n * KC : (n + 1) * KC, hs], local_putter(dvl_ref, n), carry)
        out, delta = carry
        delta = jnp.sum(delta, axis=0, keepdims=True)
        att_ref[rows, :] = out.T.astype(jnp.bfloat16)
        dq = lax.fori_loop(0, NSPLIT, mem_backward, jnp.zeros((HD, QT), jnp.float32))
        for n in range(local):
            at = slice(keys + n * KC, keys + (n + 1) * KC)
            dq = backward(at, k_ref[n * KC : (n + 1) * KC, hs], local_putter(dkl_ref, n), dq)
        gq_ref[rows, :] = dq.T.astype(jnp.bfloat16)
    ends = [
        pltpu.make_async_copy(src, dst.at[:, pl.ds(h * HD, HD)], end_sem.at[i])
        for i, (src, dst) in enumerate(((att_ref, att_hbm), (gq_ref, gq_hbm)))
    ]
    for copy in ends:
        copy.start()
    dkb[...] = dka[...].astype(jnp.bfloat16)
    dvb[...] = dva[...].astype(jnp.bfloat16)
    for w in range(NSEQ):
        for r in range(2):
            place = jnp.minimum(table_ref[(2 + r) * NSEQ, w], POOL - 1)
            for kind, ref in ((0, dkb), (1, dvb)):
                pltpu.make_async_copy(
                    ref.at[pl.ds(pl.multiple_of(place * BLK, BLK), BLK), :],
                    back_ref.at[w, kind * 2 + r],
                    out_sem,
                ).start()
    pltpu.make_async_copy(back_ref, back_ref, out_sem).wait()
    for copy in ends:
        copy.wait()


def attend(h, where, table, bias, q, do, k, v, mask, pieces_k, pieces_v, srcs, done):
    bf, f32, vm, hbm, sm = jnp.bfloat16, jnp.float32, pltpu.VMEM, pl.ANY, pltpu.SMEM
    spec = lambda space: pl.BlockSpec(memory_space=space)
    keys = POOL * BLK
    extra = list(done)
    return pl.pallas_call(
        lambda *refs: attend_kernel(h, *refs),
        in_specs=[spec(sm)] * 3 + [spec(vm)] * 5 + [spec(hbm)] * (22 + len(extra)),
        out_specs=[spec(hbm)] * 2 + [spec(vm)] * 2 + [spec(hbm)],
        out_shape=[
            jax.ShapeDtypeStruct((SEG, FEAT), bf),
            jax.ShapeDtypeStruct((SEG, FEAT), bf),
            jax.ShapeDtypeStruct((SEG, HD), f32),
            jax.ShapeDtypeStruct((SEG, HD), f32),
            jax.ShapeDtypeStruct((NSEQ, 4, BLK, HD), bf),
        ],
        scratch_shapes=[
            pltpu.VMEM((96 * BLK, HD), bf),
            pltpu.VMEM((96 * BLK, HD), bf),
            pltpu.VMEM((keys + SEG, QT), f32),
            pltpu.VMEM((keys + SEG, QT), f32),
            pltpu.VMEM((NSPLIT, SPC, SEG), f32),
            pltpu.VMEM((keys, HD), f32),
            pltpu.VMEM((keys, HD), f32),
            pltpu.VMEM((keys, HD), bf),
            pltpu.VMEM((keys, HD), bf),
            pltpu.VMEM((SEG, HD), bf),
            pltpu.VMEM((SEG, HD), bf),
            pltpu.SemaphoreType.DMA((2,)),
            pltpu.SemaphoreType.DMA,
            pltpu.SemaphoreType.DMA((2,)),
        ],
        input_output_aliases={30: 0, 31: 1} if extra else {},
        cost_estimate=pl.CostEstimate(flops=16_000_000_000, bytes_accessed=8 << 20, transcendentals=1_500_000),
    )(where, table, bias, q, do, k, v, mask, *pieces_k, *pieces_v, *srcs, *extra)


def settle_kernel(h, where_ref, table_ref, dkl_ref, dvl_ref, back_ref, *refs):
    gk_hbm, gv_hbm, dk, dv, dkb, dvb, sems = refs[2 * h :]
    me = where_ref[0]
    dk[...] = dkl_ref[...]
    dv[...] = dvl_ref[...]

    def step(s, _):
        for r in range(2):
            block = table_ref[r * NSEQ + order_of(me, s // 8, (s // 2) % 4, s % 2), me]

            @pl.when(block >= 0)
            def _():
                at = pl.ds(pl.multiple_of(block * BLK, BLK), BLK)
                dk[at, :] += back_ref[s, r].astype(jnp.float32)
                dv[at, :] += back_ref[s, 2 + r].astype(jnp.float32)

        return 0

    lax.fori_loop(0, NSEQ, step, 0)
    dkb[...] = dk[...].astype(jnp.bfloat16)
    dvb[...] = dv[...].astype(jnp.bfloat16)
    ends = [
        pltpu.make_async_copy(src, dst.at[:, pl.ds(h * HD, HD)], sems.at[i])
        for i, (src, dst) in enumerate(((dkb, gk_hbm), (dvb, gv_hbm)))
    ]
    for copy in ends:
        copy.start()
    for copy in ends:
        copy.wait()


def settle(h, where, table, dkl, dvl, back, done):
    spec = lambda space: pl.BlockSpec(memory_space=space)
    extra = list(done)
    return pl.pallas_call(
        lambda *refs: settle_kernel(h, *refs),
        in_specs=[spec(pltpu.SMEM)] * 2 + [spec(pltpu.VMEM)] * 3 + [spec(pl.ANY)] * len(extra),
        out_specs=[spec(pl.ANY)] * 2,
        out_shape=[jax.ShapeDtypeStruct((SEG, FEAT), jnp.bfloat16)] * 2,
        scratch_shapes=[pltpu.VMEM((SEG, HD), jnp.float32)] * 2
        + [pltpu.VMEM((SEG, HD), jnp.bfloat16)] * 2
        + [pltpu.SemaphoreType.DMA((2,))],
        input_output_aliases={5: 0, 6: 1} if extra else {},
        cost_estimate=pl.CostEstimate(flops=2_000_000, bytes_accessed=3 << 20, transcendentals=0),
    )(where, table, dkl, dvl, back, *extra)


def layer(queries, keys, values, grad_out, retrieved, mem_bias):
    where = jnp.stack([lax.axis_index("seq"), lax.axis_index("head")]).astype(jnp.int32)
    lists = retrieved
    for bit in (1, 2, 4):
        other = lax.ppermute(lists, "head", [(i, i ^ bit) for i in range(8)])
        lists = jnp.concatenate([lists, other], axis=1)
    for bit in (2, 4, 8, 16, 1):
        other = lax.ppermute(lists, "seq", [(i, i ^ bit) for i in range(NSEQ)])
        lists = jnp.concatenate([lists, other], axis=0)
    table, mask = prep(where, lists)
    col_k = [keys] + [shift(keys, -d, 0, 0) for d in OFFS[1:]]
    row_v = [values] + [shift(values, 0, -d, 0) for d in OFFS[1:]]
    pieces_k = [p for piece in col_k for p in (piece, shift(piece, 0, 0, 1))]
    pieces_v = [p for piece in row_v for p in (piece, shift(piece, 0, 0, 1))]
    msgs = select(where, table, pieces_k, pieces_v)
    near_k, near_v = shift(msgs[8], 0, -1, 0), shift(msgs[11], -1, 0, 0)
    fetched = []
    for h in range(2):
        kp, km, k2, vp, vm, v2 = msgs[h * 6 : h * 6 + 6]
        if h == 0:
            far_k, far_v = shift(k2, 0, 2, 0), shift(v2, 2, 0, 0)
        else:
            far_k, far_v = shift(near_k, 0, -1, 0), shift(near_v, -1, 0, 0)
        fetched.append(
            [
                shift(km, 0, -1, 0),
                shift(kp, 0, 1, 0),
                far_k,
                shift(vm, -1, 0, 0),
                shift(vp, 1, 0, 0),
                far_v,
            ]
        )
    rows, grads = (), ()
    parts = []
    for h in range(2):
        *rows, dkl, dvl, back = attend(
            h, where, table, mem_bias, queries, grad_out, keys, values, mask, pieces_k, pieces_v, fetched[h], rows
        )
        back = lax.all_to_all(back, "seq", split_axis=0, concat_axis=0, tiled=True)
        parts.append((dkl, dvl, back))
    for h in range(2):
        grads = settle(h, where, table, *parts[h], grads)
    return *rows, *grads


def solution(mesh):
    whole = P("seq", "head")
    return jax.shard_map(
        layer,
        mesh=mesh,
        in_specs=(whole, whole, whole, whole, P(("seq", "head"), None), P("head")),
        out_specs=(whole, whole, whole, whole),
        check_vma=False,
    )
```

```python
import math

import jax
import jax.numpy as jnp
from jax import lax
from jax.experimental import pallas as pl
from jax.experimental.pallas import tpu as pltpu
from jax.sharding import PartitionSpec as P

BLK = 64
NSEQ = 32
HD = 128
SEG = 512
POOL = 32
LOG2E = 1.4426950408889634
SCALE = 1.0 / math.sqrt(HD)
QT = 512
KC = 256
SPC = KC // BLK
TILES = 96
COUNT_ROW = 128
TABLE_ROWS = 136


def dot(a, b, dims):
    return lax.dot_general(a, b, (dims, ((), ())), preferred_element_type=jnp.float32)


NN = ((1,), (0,))
NT = ((1,), (1,))
TN = ((0,), (0,))


def iota(shape, dim):
    return lax.broadcasted_iota(jnp.int32, shape, dim)


def flag(cond):
    return jnp.where(cond, 1.0, 0.0)


def prep_kernel(where_ref, rows_ref, table_ref, mask_ref, named_ref, prefix_ref, wanted_ref):
    me = where_ref[0]
    nid = NSEQ * 8
    bf = jnp.bfloat16
    row, col = iota((nid, nid), 0), iota((nid, nid), 1)
    named = row < 0
    for e in range(16):
        named = named | (rows_ref[:, e : e + 1] == col)
    named = flag(named)
    named_ref[...] = named
    pick = flag(iota((NSEQ, nid), 0) == (iota((NSEQ, nid), 1) >> 3))
    wanted = flag(dot(pick.astype(bf), named.astype(bf), NN) > 0.5)
    upto = flag(row <= col)
    upto8 = flag((row <= col) & ((row >> 3) == (col >> 3)))
    prefix = dot(wanted.astype(bf), upto.astype(bf), NN)
    prefix8 = dot(wanted.astype(bf), upto8.astype(bf), NN)
    gid, gw = iota((nid, NSEQ), 0), iota((nid, NSEQ), 1)
    same = (gid >> 3) == gw
    ones = flag(same).astype(bf)
    inner = jnp.where(same, (gid & 7).astype(jnp.float32), 0.0).astype(bf)
    for r in range(2):
        picked = jnp.where(prefix8 == float(r + 1), wanted, 0.0)
        has = dot(picked.astype(bf), ones, NN)
        block = dot(picked.astype(bf), inner, NN)
        place = dot((picked * (prefix - 1.0)).astype(bf), ones, NN)
        table_ref[r * NSEQ : (r + 1) * NSEQ, :] = jnp.where(has > 0.5, block, -1.0).astype(jnp.int32)
        spare = iota((NSEQ, NSEQ), 1) + POOL + NSEQ * r
        table_ref[(2 + r) * NSEQ : (3 + r) * NSEQ, :] = jnp.where(has > 0.5, place.astype(jnp.int32), spare)
    prefix_ref[...] = jnp.where(wanted > 0.5, prefix - 1.0, -1.0)
    wanted_ref[...] = wanted
    spread = flag(iota((8, SEG), 0) == (iota((8, SEG), 1) >> 6))
    ids8, row8 = iota((8, nid), 1), iota((8, nid), 0)
    for h in range(2):
        seg = me if h == 0 else NSEQ - 1 - me
        compact = flag(iota((POOL, nid), 0).astype(jnp.float32) == prefix_ref[pl.ds(seg, 1), :])
        used = jnp.where(ids8 < seg * 8 + row8, named_ref[pl.ds(pl.multiple_of(seg * 8, 8), 8), :], 0.0)
        by_id = dot(used.astype(bf), spread.astype(bf), TN)
        mask_ref[h] = dot(compact.astype(bf), by_id.astype(bf), NN)
        held = jnp.where(iota((1, nid), 1) < seg * 8 + 8, wanted_ref[pl.ds(seg, 1), :], 0.0)
        count = jnp.sum(held, axis=1, keepdims=True)
        table_ref[COUNT_ROW + h : COUNT_ROW + h + 1, :] = jnp.broadcast_to(count, (1, NSEQ)).astype(jnp.int32)


def prep(where, rows):
    return pl.pallas_call(
        prep_kernel,
        name="prep",
        in_specs=[pl.BlockSpec(memory_space=pltpu.SMEM), pl.BlockSpec(memory_space=pltpu.VMEM)],
        out_specs=[pl.BlockSpec(memory_space=pltpu.VMEM)] * 2,
        out_shape=[
            jax.ShapeDtypeStruct((TABLE_ROWS, NSEQ), jnp.int32),
            jax.ShapeDtypeStruct((2, POOL, SEG), jnp.float32),
        ],
        scratch_shapes=[
            pltpu.VMEM((NSEQ * 8, NSEQ * 8), jnp.float32),
            pltpu.VMEM((NSEQ, NSEQ * 8), jnp.float32),
            pltpu.VMEM((NSEQ, NSEQ * 8), jnp.float32),
        ],
        cost_estimate=pl.CostEstimate(flops=10_000_000, bytes_accessed=1 << 20, transcendentals=0),
    )(where, rows)


def tile(index):
    return pl.ds(pl.multiple_of(index * BLK, BLK), BLK)


def select_kernel(where_ref, table_ref, k_ref, v_ref, far_ref, send_ref, sem):
    me = where_ref[0]

    def step(u, _):
        first = u >= me
        reader = jnp.where(first, u, NSEQ - 1 - u)
        writer = jnp.where(first, me, NSEQ - 1 - me)
        for r in range(2):
            rows = tile(jnp.maximum(table_ref[r * NSEQ + reader, writer], 0))

            @pl.when(first)
            def _():
                for kind, ref in ((0, k_ref), (1, v_ref)):
                    pltpu.make_async_copy(ref.at[rows, pl.ds(0, HD)], send_ref.at[u, kind * 2 + r], sem).start()

            @pl.when(jnp.logical_not(first))
            def _():
                for kind in range(2):
                    pltpu.make_async_copy(far_ref.at[kind, rows, :], send_ref.at[u, kind * 2 + r], sem).start()

        return 0

    lax.fori_loop(0, NSEQ, step, 0, unroll=4)
    pltpu.make_async_copy(send_ref, send_ref, sem).wait()


def select(where, table, k, v, far):
    spec = lambda space: pl.BlockSpec(memory_space=space)
    return pl.pallas_call(
        select_kernel,
        name="select",
        in_specs=[spec(pltpu.SMEM)] * 2 + [spec(pltpu.VMEM)] * 3,
        out_specs=spec(pl.ANY),
        out_shape=jax.ShapeDtypeStruct((NSEQ, 4, BLK, HD), jnp.bfloat16),
        scratch_shapes=[pltpu.SemaphoreType.DMA],
        cost_estimate=pl.CostEstimate(flops=1_000_000, bytes_accessed=3 << 20, transcendentals=0),
    )(where, table, k, v, far)


def attend_kernel(where_ref, table_ref, bias_ref, *refs):
    q_ref, do_ref, k_ref, v_ref, far_kv_ref, far_q_ref, mask_ref, got_ref = refs[:8]
    outs, back_ref = refs[8:16], refs[16]
    kt, vt, s_ref, dp_ref, add_ref, dka, dva, dkb, dvb, sems, out_sem = refs[17:]
    me = where_ref[0]
    keys = POOL * BLK
    tiles = (kt, vt)
    segs = (me, NSEQ - 1 - me)

    def fetch(u, _):
        first = u < me
        h = jnp.where(first, 0, 1)
        seg = jnp.where(first, segs[0], segs[1])
        writer = jnp.where(first, u, NSEQ - 1 - u)

        @pl.when(u != me)
        def _():
            for r in range(2):
                at = tile(h * TILES + table_ref[(2 + r) * NSEQ + seg, writer])
                for kind in range(2):
                    pltpu.make_async_copy(
                        got_ref.at[u, kind * 2 + r], tiles[kind].at[at, :], sems.at[kind]
                    ).start()

        return 0

    lax.fori_loop(0, NSEQ, fetch, 0, unroll=4)
    heads = []
    for h in range(2):
        if h == 0:
            lanes = slice(0, HD)
            q, do, k, v = (r.at[:, lanes] for r in (q_ref, do_ref, k_ref, v_ref))
        else:
            q, do, k, v = far_q_ref.at[0], far_q_ref.at[1], far_kv_ref.at[0], far_kv_ref.at[1]
        heads.append((q, do, k, v))
        held = table_ref[COUNT_ROW + h, 0]
        for r in range(2):
            rows = tile(jnp.maximum(table_ref[r * NSEQ + segs[h], segs[h]], 0))
            at = tile(h * TILES + table_ref[(2 + r) * NSEQ + segs[h], segs[h]])
            kt[at, :] = k[rows, :]
            vt[at, :] = v[rows, :]

        def clear(i, _):
            at = tile(h * TILES + i)
            kt[at, :] = jnp.zeros((BLK, HD), jnp.bfloat16)
            vt[at, :] = jnp.zeros((BLK, HD), jnp.bfloat16)
            return 0

        lax.fori_loop(held, (held + SPC - 1) // SPC * SPC, clear, 0)
        for i in range(POOL // SPC):
            add_ref[h, i] = jnp.where(mask_ref[h, i * SPC : (i + 1) * SPC, :] > 0.5, bias_ref[h] * LOG2E, -1e30)
    for kind in range(2):
        most = tiles[kind].at[pl.ds(0, 2 * (NSEQ - 1) * BLK), :]
        pltpu.make_async_copy(most, most, sems.at[kind]).wait()

    def fold(value, op):
        return op(value.reshape(KC // 8, 8, QT), axis=0)

    for h in range(2):
        q, do, k, v = heads[h]
        att_ref, gq_ref, dkl_ref, dvl_ref = outs[h * 4 : h * 4 + 4]
        steps = (table_ref[COUNT_ROW + h, 0] + SPC - 1) // SPC
        qc, doc = q[...], do[...]

        def chunk(i):
            return pl.ds(pl.multiple_of(i * KC, KC), KC)

        def held_chunk(i):
            return pl.ds(pl.multiple_of(h * TILES * BLK + i * KC, KC), KC)

        def mem_score(i, top):
            score = dot(kt[held_chunk(i), :], qc, NT) * (SCALE * LOG2E)
            add = add_ref[h, i]
            score = (score.reshape(SPC, BLK, QT) + add[:, None, :]).reshape(KC, QT)
            s_ref[chunk(i), :] = score
            return jnp.maximum(top, fold(score, jnp.max))

        top = jnp.full((8, QT), -1e30, jnp.float32)
        for n in range(SEG // KC):
            score = dot(k[n * KC : (n + 1) * KC, :], qc, NT) * (SCALE * LOG2E)
            score = jnp.where(iota((KC, QT), 0) + n * KC <= iota((KC, QT), 1), score, -1e30)
            s_ref[keys + n * KC : keys + (n + 1) * KC, :] = score
            top = jnp.maximum(top, fold(score, jnp.max))
        top = lax.fori_loop(0, steps, mem_score, top)
        top = jnp.max(top, axis=0, keepdims=True)

        def weigh(i, mass):
            e = jnp.exp2(s_ref[chunk(i), :] - top)
            s_ref[chunk(i), :] = e
            return mass + fold(e, jnp.sum)

        mass = lax.fori_loop(0, steps, weigh, jnp.zeros((8, QT), jnp.float32))
        mass = lax.fori_loop(POOL // SPC, POOL // SPC + SEG // KC, weigh, mass)
        inv = 1.0 / jnp.sum(mass, axis=0, keepdims=True)

        def forward(at, vc, carry):
            out, delta = carry
            p = s_ref[at, :] * inv
            s_ref[at, :] = p
            w = p.astype(jnp.bfloat16)
            out = out + dot(vc, w, TN)
            dp = dot(vc, doc, NT)
            dp_ref[at, :] = dp
            return dot(w, doc, NN), (out, delta + fold(p * dp, jnp.sum))

        def backward(at, kc, dq):
            ds = (s_ref[at, :] * (dp_ref[at, :] - delta) * SCALE).astype(jnp.bfloat16)
            return dot(ds, qc, NN), dq + dot(kc, ds, TN)

        def mem_forward(i, carry):
            dva[chunk(i), :], carry = forward(chunk(i), vt[held_chunk(i), :], carry)
            return carry

        def mem_backward(i, dq):
            dka[chunk(i), :], dq = backward(chunk(i), kt[held_chunk(i), :], dq)
            return dq

        carry = (jnp.zeros((HD, QT), jnp.float32), jnp.zeros((8, QT), jnp.float32))
        carry = lax.fori_loop(0, steps, mem_forward, carry)
        for n in range(SEG // KC):
            rows = slice(n * KC, (n + 1) * KC)
            at = slice(keys + n * KC, keys + (n + 1) * KC)
            dvl_ref[rows, :], carry = forward(at, v[rows, :], carry)
        out, delta = carry
        delta = jnp.sum(delta, axis=0, keepdims=True)
        att_ref[...] = out.T.astype(jnp.bfloat16)
        dq = lax.fori_loop(0, steps, mem_backward, jnp.zeros((HD, QT), jnp.float32))
        for n in range(SEG // KC):
            rows = slice(n * KC, (n + 1) * KC)
            at = slice(keys + n * KC, keys + (n + 1) * KC)
            dkl_ref[rows, :], dq = backward(at, k[rows, :], dq)
        gq_ref[...] = dq.T.astype(jnp.bfloat16)

        def pack(i, _):
            dkb[h, chunk(i), :] = dka[chunk(i), :].astype(jnp.bfloat16)
            dvb[h, chunk(i), :] = dva[chunk(i), :].astype(jnp.bfloat16)
            return 0

        lax.fori_loop(0, steps, pack, 0)
        for r in range(2):
            block = table_ref[r * NSEQ + segs[h], segs[h]]

            @pl.when(block >= 0)
            def _():
                rows, at = tile(block), tile(table_ref[(2 + r) * NSEQ + segs[h], segs[h]])
                dkl_ref[rows, :] += dkb[h, at, :].astype(jnp.float32)
                dvl_ref[rows, :] += dvb[h, at, :].astype(jnp.float32)

        def put(u, _):
            writer = u if h == 0 else NSEQ - 1 - u
            for r in range(2):
                at = tile(jnp.minimum(table_ref[(2 + r) * NSEQ + segs[h], writer], POOL - 1))
                for kind, ref in ((0, dkb), (1, dvb)):
                    pltpu.make_async_copy(ref.at[h, at, :], back_ref.at[u, kind * 2 + r], out_sem).start()
            return 0

        lax.fori_loop(*((0, me + 1) if h == 0 else (me + 1, NSEQ)), put, 0)
    pltpu.make_async_copy(back_ref, back_ref, out_sem).wait()


def attend(where, table, bias, q, do, k, v, far_kv, far_q, mask, got):
    bf, f32, vm, hbm, sm = jnp.bfloat16, jnp.float32, pltpu.VMEM, pl.ANY, pltpu.SMEM
    spec = lambda space: pl.BlockSpec(memory_space=space)
    keys = POOL * BLK
    each = [jax.ShapeDtypeStruct((SEG, HD), d) for d in (bf, bf, f32, f32)]
    return pl.pallas_call(
        attend_kernel,
        name="attend",
        in_specs=[spec(sm)] * 3 + [spec(vm)] * 7 + [spec(hbm)],
        out_specs=[spec(vm)] * 8 + [spec(hbm)],
        out_shape=each * 2 + [jax.ShapeDtypeStruct((NSEQ, 4, BLK, HD), bf)],
        scratch_shapes=[
            pltpu.VMEM((2 * TILES * BLK, HD), bf),
            pltpu.VMEM((2 * TILES * BLK, HD), bf),
            pltpu.VMEM((keys + SEG, QT), f32),
            pltpu.VMEM((keys + SEG, QT), f32),
            pltpu.VMEM((2, POOL // SPC, SPC, SEG), f32),
            pltpu.VMEM((keys, HD), f32),
            pltpu.VMEM((keys, HD), f32),
            pltpu.VMEM((2, keys, HD), bf),
            pltpu.VMEM((2, keys, HD), bf),
            pltpu.SemaphoreType.DMA((2,)),
            pltpu.SemaphoreType.DMA,
        ],
        cost_estimate=pl.CostEstimate(flops=16_000_000_000, bytes_accessed=8 << 20, transcendentals=1_500_000),
    )(where, table, bias, q, do, k, v, far_kv, far_q, mask, got)


def settle_kernel(where_ref, table_ref, *refs):
    locals_, back_ref = refs[:4], refs[4]
    gk_ref, gv_ref, far_ref, acc = refs[5:]
    me = where_ref[0]
    for i in range(4):
        acc[i] = locals_[i][...]

    def step(u, _):
        first = u > me
        h = jnp.where(first, 0, 1)
        reader = jnp.where(first, u, NSEQ - 1 - u)
        writer = jnp.where(first, me, NSEQ - 1 - me)
        for r in range(2):
            block = table_ref[r * NSEQ + reader, writer]

            @pl.when((block >= 0) & (u != me))
            def _():
                for kind in range(2):
                    acc[h * 2 + kind, tile(block), :] += back_ref[u, kind * 2 + r].astype(jnp.float32)

        return 0

    lax.fori_loop(0, NSEQ, step, 0)
    gk_ref[...] = acc[0].astype(jnp.bfloat16)
    gv_ref[...] = acc[1].astype(jnp.bfloat16)
    far_ref[...] = acc[2:4].astype(jnp.bfloat16)


def settle(where, table, parts, back):
    spec = lambda space: pl.BlockSpec(memory_space=space)
    return pl.pallas_call(
        settle_kernel,
        name="settle",
        in_specs=[spec(pltpu.SMEM)] * 2 + [spec(pltpu.VMEM)] * 5,
        out_specs=[spec(pltpu.VMEM)] * 3,
        out_shape=[jax.ShapeDtypeStruct((SEG, HD), jnp.bfloat16)] * 2
        + [jax.ShapeDtypeStruct((2, SEG, HD), jnp.bfloat16)],
        scratch_shapes=[pltpu.VMEM((4, SEG, HD), jnp.float32)],
        cost_estimate=pl.CostEstimate(flops=2_000_000, bytes_accessed=3 << 20, transcendentals=0),
    )(where, table, *parts, back)


def mirror(first, second):
    pairs = [(i, NSEQ - 1 - i) for i in range(NSEQ)]
    return lax.ppermute(jnp.stack([first, second]), "seq", pairs)


def exchange(value):
    return lax.all_to_all(value, "seq", split_axis=0, concat_axis=0, tiled=True)


def layer(queries, keys, values, grad_out, retrieved, mem_bias):
    where = lax.axis_index("seq").astype(jnp.int32).reshape(1)
    devices = lax.axis_size("seq") * lax.axis_size("head")
    far_kv = mirror(keys[:, HD:], values[:, HD:])
    copies = jnp.broadcast_to(retrieved, (devices, *retrieved.shape))
    lists = lax.all_to_all(copies, ("seq", "head"), split_axis=0, concat_axis=0, tiled=True)
    far_q = mirror(queries[:, HD:], grad_out[:, HD:])
    table, mask = prep(where, lists.reshape(devices, 16))
    send = select(where, table, keys, values, far_kv)
    got = exchange(send)
    att, gq, dkl, dvl, far_att, far_gq, far_dkl, far_dvl, back = attend(
        where, table, mem_bias, queries, grad_out, keys, values, far_kv, far_q, mask, got
    )
    home = mirror(far_att, far_gq)
    attended = jnp.concatenate([att, home[0]], axis=1)
    grad_queries = jnp.concatenate([gq, home[1]], axis=1)
    back = exchange(back)
    gk, gv, far = settle(where, table, (dkl, dvl, far_dkl, far_dvl), back)
    far = lax.ppermute(far, "seq", [(i, NSEQ - 1 - i) for i in range(NSEQ)])
    grad_keys = jnp.concatenate([gk, far[0]], axis=1)
    grad_values = jnp.concatenate([gv, far[1]], axis=1)
    return attended, grad_queries, grad_keys, grad_values


def solution(mesh):
    whole = P("seq", "head")
    return jax.shard_map(
        layer,
        mesh=mesh,
        in_specs=(whole, whole, whole, whole, P(("seq", "head"), None), P("head")),
        out_specs=(whole, whole, whole, whole),
        check_vma=False,
    )
```

```python
import math

import jax
import jax.numpy as jnp
from jax import lax
from jax.experimental import pallas as pl
from jax.experimental.pallas import tpu as pltpu
from jax.sharding import PartitionSpec as P


BLK = 64
NSEQ = 32
HD = 128
SEG = 512
POOL = 32
LOG2E = 1.4426950408889634
SCALE = 1.0 / math.sqrt(HD)
QT = 512
KC = 256
SPC = KC // BLK
TILES = 96
PARTS = 8
VMEM_SETTLE = 16 << 20
COUNT_ROW = 128
TABLE_ROWS = 136


def dot(a, b, dims):
    return lax.dot_general(a, b, (dims, ((), ())), preferred_element_type=jnp.float32)


NN = ((1,), (0,))
NT = ((1,), (1,))
TN = ((0,), (0,))


def iota(shape, dim):
    return lax.broadcasted_iota(jnp.int32, shape, dim)


def flag(cond):
    return jnp.where(cond, 1.0, 0.0)


def tile(index):
    return pl.ds(pl.multiple_of(index * BLK, BLK), BLK)


def select_kernel(where_ref, rows_ref, upto_ref, upto8_ref, k_ref, v_ref, far_ref, *refs):
    table_ref, mask_ref, send_ref, table, named_ref, prefix_ref, wanted_ref, table_sem, sem = refs
    me = where_ref[0]
    nid = NSEQ * 8
    bf = jnp.bfloat16
    col = iota((nid, nid), 1)
    named = col < 0
    for e in range(16):
        named = named | (rows_ref[:, e : e + 1] == col)
    named = flag(named)
    named_ref[...] = named
    pick = flag(iota((NSEQ, nid), 0) == (iota((NSEQ, nid), 1) >> 3))
    wanted = flag(dot(pick.astype(bf), named.astype(bf), NN) > 0.5)
    prefix = dot(wanted.astype(bf), upto_ref[...], NN)
    prefix8 = dot(wanted.astype(bf), upto8_ref[...], NN)
    gid, gw = iota((nid, NSEQ), 0), iota((nid, NSEQ), 1)
    same = (gid >> 3) == gw
    ones = flag(same).astype(bf)
    inner = jnp.where(same, (gid & 7).astype(jnp.float32), 0.0).astype(bf)
    places = []
    for r in range(2):
        picked = jnp.where(prefix8 == float(r + 1), wanted, 0.0)
        has = dot(picked.astype(bf), ones, NN)
        block = dot(picked.astype(bf), inner, NN)
        table_ref[r * NSEQ : (r + 1) * NSEQ, :] = jnp.where(has > 0.5, block, -1.0).astype(jnp.int32)
        places.append((picked, has))
    to_smem = pltpu.make_async_copy(table_ref.at[pl.ds(0, 2 * NSEQ), :], table, table_sem)
    to_smem.start()
    for r, (picked, has) in enumerate(places):
        place = dot((picked * (prefix - 1.0)).astype(bf), ones, NN)
        spare = iota((NSEQ, NSEQ), 1) + POOL + NSEQ * r
        table_ref[(2 + r) * NSEQ : (3 + r) * NSEQ, :] = jnp.where(has > 0.5, place.astype(jnp.int32), spare)
    prefix_ref[...] = jnp.where(wanted > 0.5, prefix - 1.0, -1.0)
    wanted_ref[...] = wanted
    to_smem.wait()

    def step(u, _):
        first = u >= me
        reader = jnp.where(first, u, NSEQ - 1 - u)
        writer = jnp.where(first, me, NSEQ - 1 - me)
        for r in range(2):
            rows = tile(jnp.maximum(table[r * NSEQ + reader, writer], 0))

            @pl.when(first)
            def _():
                for kind, ref in ((0, k_ref), (1, v_ref)):
                    pltpu.make_async_copy(ref.at[rows, pl.ds(0, HD)], send_ref.at[u, kind * 2 + r], sem).start()

            @pl.when(jnp.logical_not(first))
            def _():
                for kind in range(2):
                    pltpu.make_async_copy(far_ref.at[kind, rows, :], send_ref.at[u, kind * 2 + r], sem).start()

        return 0

    lax.fori_loop(0, NSEQ, step, 0, unroll=4)
    spread = flag(iota((8, SEG), 0) == (iota((8, SEG), 1) >> 6))
    ids8, row8 = iota((8, nid), 1), iota((8, nid), 0)
    for h in range(2):
        seg = me if h == 0 else NSEQ - 1 - me
        compact = flag(iota((POOL, nid), 0).astype(jnp.float32) == prefix_ref[pl.ds(seg, 1), :])
        used = jnp.where(ids8 < seg * 8 + row8, named_ref[pl.ds(pl.multiple_of(seg * 8, 8), 8), :], 0.0)
        by_id = dot(used.astype(bf), spread.astype(bf), TN)
        mask_ref[h] = dot(compact.astype(bf), by_id.astype(bf), NN)
        held = jnp.where(iota((1, nid), 1) < seg * 8 + 8, wanted_ref[pl.ds(seg, 1), :], 0.0)
        count = jnp.sum(held, axis=1, keepdims=True)
        table_ref[COUNT_ROW + h : COUNT_ROW + h + 1, :] = jnp.broadcast_to(count, (1, NSEQ)).astype(jnp.int32)
    pltpu.make_async_copy(send_ref, send_ref, sem).wait()


def select(where, rows, k, v, far):
    spec = lambda space: pl.BlockSpec(memory_space=space)
    nid = NSEQ * 8
    row, col = iota((nid, nid), 0), iota((nid, nid), 1)
    upto = (row <= col).astype(jnp.bfloat16)
    upto8 = ((row <= col) & ((row >> 3) == (col >> 3))).astype(jnp.bfloat16)
    return pl.pallas_call(
        select_kernel,
        name="select",
        in_specs=[spec(pltpu.SMEM)] + [spec(pltpu.VMEM)] * 6,
        out_specs=[spec(pltpu.VMEM)] * 2 + [spec(pl.ANY)],
        out_shape=[
            jax.ShapeDtypeStruct((TABLE_ROWS, NSEQ), jnp.int32),
            jax.ShapeDtypeStruct((2, POOL, SEG), jnp.float32),
            jax.ShapeDtypeStruct((NSEQ, 4, BLK, HD), jnp.bfloat16),
        ],
        scratch_shapes=[
            pltpu.SMEM((2 * NSEQ, NSEQ), jnp.int32),
            pltpu.VMEM((nid, nid), jnp.float32),
            pltpu.VMEM((NSEQ, nid), jnp.float32),
            pltpu.VMEM((NSEQ, nid), jnp.float32),
            pltpu.SemaphoreType.DMA,
            pltpu.SemaphoreType.DMA,
        ],
        cost_estimate=pl.CostEstimate(flops=10_000_000, bytes_accessed=4 << 20, transcendentals=0),
    )(where, rows, upto, upto8, k, v, far)


def attend_kernel(where_ref, table_ref, bias_ref, *refs):
    q_ref, do_ref, k_ref, v_ref, far_kv_ref, far_q_ref, mask_ref, got_ref = refs[:8]
    outs, back_ref = refs[8:16], refs[16]
    kt, vt, s_ref, dp_ref, add_ref, dka, dva, dkb, dvb, sems, out_sem = refs[17:]
    me = where_ref[0]
    keys = POOL * BLK
    tiles = (kt, vt)
    segs = (me, NSEQ - 1 - me)

    def fetch(u, _):
        first = u < me
        h = jnp.where(first, 0, 1)
        seg = jnp.where(first, segs[0], segs[1])
        writer = jnp.where(first, u, NSEQ - 1 - u)

        @pl.when(u != me)
        def _():
            for r in range(2):
                at = tile(h * TILES + table_ref[(2 + r) * NSEQ + seg, writer])
                for kind in range(2):
                    pltpu.make_async_copy(
                        got_ref.at[u, kind * 2 + r], tiles[kind].at[at, :], sems.at[kind]
                    ).start()

        return 0

    lax.fori_loop(0, NSEQ, fetch, 0, unroll=4)
    heads = []
    for h in range(2):
        if h == 0:
            lanes = slice(0, HD)
            q, do, k, v = (r.at[:, lanes] for r in (q_ref, do_ref, k_ref, v_ref))
        else:
            q, do, k, v = far_q_ref.at[0], far_q_ref.at[1], far_kv_ref.at[0], far_kv_ref.at[1]
        heads.append((q, do, k, v))
        held = table_ref[COUNT_ROW + h, 0]
        for r in range(2):
            rows = tile(jnp.maximum(table_ref[r * NSEQ + segs[h], segs[h]], 0))
            at = tile(h * TILES + table_ref[(2 + r) * NSEQ + segs[h], segs[h]])
            kt[at, :] = k[rows, :]
            vt[at, :] = v[rows, :]

        def clear(i, _):
            at = tile(h * TILES + i)
            kt[at, :] = jnp.zeros((BLK, HD), jnp.bfloat16)
            vt[at, :] = jnp.zeros((BLK, HD), jnp.bfloat16)
            return 0

        lax.fori_loop(held, (held + SPC - 1) // SPC * SPC, clear, 0)
        for i in range(POOL // SPC):
            add_ref[h, i] = jnp.where(mask_ref[h, i * SPC : (i + 1) * SPC, :] > 0.5, bias_ref[h] * LOG2E, -1e30)

    def fold(value, op):
        return op(value.reshape(KC // 8, 8, value.shape[1]), axis=0)

    def merge(total, value, op):
        lo = total.shape[1] - value.shape[1]
        late = op(total[:, lo:], value)
        return late if lo == 0 else jnp.concatenate([total[:, :lo], late], axis=1)

    for h in range(2):
        q, do, k, v = heads[h]
        att_ref, gq_ref, dkl_ref, dvl_ref = outs[h * 4 : h * 4 + 4]
        steps = (table_ref[COUNT_ROW + h, 0] + SPC - 1) // SPC
        qc, doc = q[...], do[...]

        def chunk(i):
            return pl.ds(pl.multiple_of(i * KC, KC), KC)

        def held_chunk(i):
            return pl.ds(pl.multiple_of(h * TILES * BLK + i * KC, KC), KC)

        def mem_score(i, top):
            score = dot(kt[held_chunk(i), :], qc, NT) * (SCALE * LOG2E)
            add = add_ref[h, i]
            score = (score.reshape(SPC, BLK, QT) + add[:, None, :]).reshape(KC, QT)
            s_ref[chunk(i), :] = score
            return jnp.maximum(top, fold(score, jnp.max))

        top = jnp.full((8, QT), -1e30, jnp.float32)
        for n in range(SEG // KC):
            lo = n * KC
            score = dot(k[lo : lo + KC, :], qc[lo:], NT) * (SCALE * LOG2E)
            score = jnp.where(iota(score.shape, 0) <= iota(score.shape, 1), score, -1e30)
            s_ref[keys + lo : keys + lo + KC, lo:] = score
            top = merge(top, fold(score, jnp.max), jnp.maximum)
        if h == 0:
            for kind in range(2):
                most = tiles[kind].at[pl.ds(0, 2 * (NSEQ - 1) * BLK), :]
                pltpu.make_async_copy(most, most, sems.at[kind]).wait()
        top = lax.fori_loop(0, steps, mem_score, top)
        top = jnp.max(top, axis=0, keepdims=True)

        def weigh(i, mass):
            e = jnp.exp2(s_ref[chunk(i), :] - top)
            s_ref[chunk(i), :] = e
            return mass + fold(e, jnp.sum)

        mass = lax.fori_loop(0, steps, weigh, jnp.zeros((8, QT), jnp.float32))
        for lo in range(0, SEG, KC):
            at = slice(keys + lo, keys + lo + KC)
            e = jnp.exp2(s_ref[at, lo:] - top[:, lo:])
            s_ref[at, lo:] = e
            mass = merge(mass, fold(e, jnp.sum), jnp.add)
        inv = 1.0 / jnp.sum(mass, axis=0, keepdims=True)

        def forward(at, vc, carry, lo=0):
            out, delta = carry
            p = s_ref[at, lo:] * inv[:, lo:]
            s_ref[at, lo:] = p
            w = p.astype(jnp.bfloat16)
            out = merge(out, dot(vc, w, TN), jnp.add)
            dp = dot(vc, doc[lo:], NT)
            dp_ref[at, lo:] = dp
            return dot(w, doc[lo:], NN), (out, merge(delta, fold(p * dp, jnp.sum), jnp.add))

        def backward(at, kc, dq, lo=0):
            ds = (s_ref[at, lo:] * (dp_ref[at, lo:] - delta[:, lo:]) * SCALE).astype(jnp.bfloat16)
            return dot(ds, qc[lo:], NN), merge(dq, dot(kc, ds, TN), jnp.add)

        def mem_forward(i, carry):
            dva[chunk(i), :], carry = forward(chunk(i), vt[held_chunk(i), :], carry)
            return carry

        def mem_backward(i, dq):
            dka[chunk(i), :], dq = backward(chunk(i), kt[held_chunk(i), :], dq)
            return dq

        carry = (jnp.zeros((HD, QT), jnp.float32), jnp.zeros((8, QT), jnp.float32))
        carry = lax.fori_loop(0, steps, mem_forward, carry)
        for n in range(SEG // KC):
            rows = slice(n * KC, (n + 1) * KC)
            at = slice(keys + n * KC, keys + (n + 1) * KC)
            dvl_ref[rows, :], carry = forward(at, v[rows, :], carry, n * KC)
        out, delta = carry
        delta = jnp.sum(delta, axis=0, keepdims=True)
        att_ref[...] = out.T.astype(jnp.bfloat16)
        dq = lax.fori_loop(0, steps, mem_backward, jnp.zeros((HD, QT), jnp.float32))
        for n in range(SEG // KC):
            rows = slice(n * KC, (n + 1) * KC)
            at = slice(keys + n * KC, keys + (n + 1) * KC)
            dkl_ref[rows, :], dq = backward(at, k[rows, :], dq, n * KC)
        gq_ref[...] = dq.T.astype(jnp.bfloat16)

        def pack(i, _):
            dkb[h, chunk(i), :] = dka[chunk(i), :].astype(jnp.bfloat16)
            dvb[h, chunk(i), :] = dva[chunk(i), :].astype(jnp.bfloat16)
            return 0

        lax.fori_loop(0, steps, pack, 0)
        for r in range(2):
            block = table_ref[r * NSEQ + segs[h], segs[h]]

            @pl.when(block >= 0)
            def _():
                rows, at = tile(block), tile(table_ref[(2 + r) * NSEQ + segs[h], segs[h]])
                dkl_ref[rows, :] += dkb[h, at, :].astype(jnp.float32)
                dvl_ref[rows, :] += dvb[h, at, :].astype(jnp.float32)

        def put(u, _):
            writer = u if h == 0 else NSEQ - 1 - u
            for r in range(2):
                at = tile(jnp.minimum(table_ref[(2 + r) * NSEQ + segs[h], writer], POOL - 1))
                for kind, ref in ((0, dkb), (1, dvb)):
                    pltpu.make_async_copy(ref.at[h, at, :], back_ref.at[u, kind * 2 + r], out_sem).start()
            return 0

        lax.fori_loop(*((0, me + 1) if h == 0 else (me + 1, NSEQ)), put, 0)
    pltpu.make_async_copy(back_ref, back_ref, out_sem).wait()


def attend(where, table, bias, q, do, k, v, far_kv, far_q, mask, got):
    bf, f32, vm, hbm, sm = jnp.bfloat16, jnp.float32, pltpu.VMEM, pl.ANY, pltpu.SMEM
    spec = lambda space: pl.BlockSpec(memory_space=space)
    keys = POOL * BLK
    each = [jax.ShapeDtypeStruct((SEG, HD), d) for d in (bf, bf, f32, f32)]
    return pl.pallas_call(
        attend_kernel,
        name="attend",
        in_specs=[spec(sm)] * 3 + [spec(vm)] * 7 + [spec(hbm)],
        out_specs=[spec(vm)] * 8 + [spec(hbm)],
        out_shape=each * 2 + [jax.ShapeDtypeStruct((NSEQ, 4, BLK, HD), bf)],
        scratch_shapes=[
            pltpu.VMEM((2 * TILES * BLK, HD), bf),
            pltpu.VMEM((2 * TILES * BLK, HD), bf),
            pltpu.VMEM((keys + SEG, QT), f32),
            pltpu.VMEM((keys + SEG, QT), f32),
            pltpu.VMEM((2, POOL // SPC, SPC, SEG), f32),
            pltpu.VMEM((keys, HD), f32),
            pltpu.VMEM((keys, HD), f32),
            pltpu.VMEM((2, keys, HD), bf),
            pltpu.VMEM((2, keys, HD), bf),
            pltpu.SemaphoreType.DMA((2,)),
            pltpu.SemaphoreType.DMA,
        ],
        cost_estimate=pl.CostEstimate(flops=16_000_000_000, bytes_accessed=8 << 20, transcendentals=1_500_000),
    )(where, table, bias, q, do, k, v, far_kv, far_q, mask, got)


def settle_kernel(where_ref, table_ref, *refs):
    locals_, back_ref = refs[:4], refs[4]
    gk_ref, gv_ref, far_ref, acc = refs[5:]
    me = where_ref[0]
    part = pl.program_id(0)
    count = NSEQ // PARTS

    @pl.when(part == 0)
    def _():
        for i in range(4):
            acc[i] = locals_[i][...]

    def step(i, _):
        u = part * count + i
        first = u > me
        h = jnp.where(first, 0, 1)
        reader = jnp.where(first, u, NSEQ - 1 - u)
        writer = jnp.where(first, me, NSEQ - 1 - me)
        for r in range(2):
            block = table_ref[r * NSEQ + reader, writer]

            @pl.when((block >= 0) & (u != me))
            def _():
                for kind in range(2):
                    acc[h * 2 + kind, tile(block), :] += back_ref[i, kind * 2 + r].astype(jnp.float32)

        return 0

    lax.fori_loop(0, count, step, 0)

    @pl.when(part == PARTS - 1)
    def _():
        gk_ref[...] = acc[0].astype(jnp.bfloat16)
        gv_ref[...] = acc[1].astype(jnp.bfloat16)
        far_ref[...] = acc[2:4].astype(jnp.bfloat16)


def settle(where, table, parts, back):
    f32, bf = jnp.float32, jnp.bfloat16
    whole = lambda *shape: pl.BlockSpec(shape, lambda i, *_: (0,) * len(shape))
    return pl.pallas_call(
        settle_kernel,
        name="settle",
        grid_spec=pltpu.PrefetchScalarGridSpec(
            num_scalar_prefetch=2,
            grid=(PARTS,),
            in_specs=[whole(SEG, HD)] * 4
            + [pl.BlockSpec((NSEQ // PARTS, 4, BLK, HD), lambda i, *_: (i, 0, 0, 0))],
            out_specs=[whole(SEG, HD)] * 2 + [whole(2, SEG, HD)],
            scratch_shapes=[pltpu.VMEM((4, SEG, HD), f32)],
        ),
        out_shape=[jax.ShapeDtypeStruct((SEG, HD), bf)] * 2 + [jax.ShapeDtypeStruct((2, SEG, HD), bf)],
        compiler_params=pltpu.CompilerParams(vmem_limit_bytes=VMEM_SETTLE),
        cost_estimate=pl.CostEstimate(flops=2_000_000, bytes_accessed=3 << 20, transcendentals=0),
    )(where, table, *parts, back)


def mirror(first, second):
    pairs = [(i, NSEQ - 1 - i) for i in range(NSEQ)]
    return lax.ppermute(jnp.stack([first, second]), "seq", pairs)


def exchange(value):
    return lax.all_to_all(value, "seq", split_axis=0, concat_axis=0, tiled=True)


def layer(queries, keys, values, grad_out, retrieved, mem_bias):
    where = lax.axis_index("seq").astype(jnp.int32).reshape(1)
    devices = lax.axis_size("seq") * lax.axis_size("head")
    far_kv = mirror(keys[:, HD:], values[:, HD:])
    copies = jnp.broadcast_to(retrieved, (devices, *retrieved.shape))
    lists = lax.all_to_all(copies, ("seq", "head"), split_axis=0, concat_axis=0, tiled=True)
    far_q = mirror(queries[:, HD:], grad_out[:, HD:])
    table, mask, send = select(where, lists.reshape(devices, 16), keys, values, far_kv)
    got = exchange(send)
    att, gq, dkl, dvl, far_att, far_gq, far_dkl, far_dvl, back = attend(
        where, table, mem_bias, queries, grad_out, keys, values, far_kv, far_q, mask, got
    )
    home = mirror(far_att, far_gq)
    attended = jnp.concatenate([att, home[0]], axis=1)
    grad_queries = jnp.concatenate([gq, home[1]], axis=1)
    back = exchange(back)
    gk, gv, far = settle(where, table, (dkl, dvl, far_dkl, far_dvl), back)
    far = lax.ppermute(far, "seq", [(i, NSEQ - 1 - i) for i in range(NSEQ)])
    grad_keys = jnp.concatenate([gk, far[0]], axis=1)
    grad_values = jnp.concatenate([gv, far[1]], axis=1)
    return attended, grad_queries, grad_keys, grad_values


def solution(mesh):
    whole = P("seq", "head")
    return jax.shard_map(
        layer,
        mesh=mesh,
        in_specs=(whole, whole, whole, whole, P(("seq", "head"), None), P("head")),
        out_specs=(whole, whole, whole, whole),
        check_vma=False,
    )
```

```python
import math

import jax
import jax.numpy as jnp
from jax import lax
from jax.experimental import pallas as pl
from jax.experimental.pallas import tpu as pltpu
from jax.sharding import PartitionSpec as P


BLK = 64
NSEQ = 32
HD = 128
SEG = 512
POOL = 32
LOG2E = 1.4426950408889634
SCALE = 1.0 / math.sqrt(HD)
QT = 512
KC = 256
SPC = KC // BLK
TILES = 96
PARTS = 8
VMEM_SETTLE = 16 << 20
COUNT_ROW = 128
TABLE_ROWS = 136


def dot(a, b, dims):
    return lax.dot_general(a, b, (dims, ((), ())), preferred_element_type=jnp.float32)


NN = ((1,), (0,))
NT = ((1,), (1,))
TN = ((0,), (0,))


def iota(shape, dim):
    return lax.broadcasted_iota(jnp.int32, shape, dim)


def flag(cond):
    return jnp.where(cond, 1.0, 0.0)


def tile(index):
    return pl.ds(pl.multiple_of(index * BLK, BLK), BLK)


def names(rows_ref):
    nid = NSEQ * 8
    col = iota((nid, nid), 1)
    named = col < 0
    for e in range(16):
        named = named | (rows_ref[:, e : e + 1] == col)
    named = flag(named)
    pick = flag(iota((NSEQ, nid), 0) == (iota((NSEQ, nid), 1) >> 3)).astype(jnp.bfloat16)
    return named, flag(dot(pick, named.astype(jnp.bfloat16), NN) > 0.5)


def owners():
    gid, gw = iota((NSEQ * 8, NSEQ), 0), iota((NSEQ * 8, NSEQ), 1)
    return (gid >> 3) == gw, (gid & 7).astype(jnp.float32)


def select_kernel(where_ref, rows_ref, upto8_ref, k_ref, v_ref, far_ref, *refs):
    table_ref, send_ref, table, table_sem, sem = refs
    me = where_ref[0]
    bf = jnp.bfloat16
    _, wanted = names(rows_ref)
    prefix8 = dot(wanted.astype(bf), upto8_ref[...], NN)
    same, inner = owners()
    inner = jnp.where(same, inner + 1.0, 0.0).astype(bf)
    for r in range(2):
        picked = jnp.where(prefix8 == float(r + 1), wanted, 0.0)
        table_ref[r * NSEQ : (r + 1) * NSEQ, :] = dot(picked.astype(bf), inner, NN).astype(jnp.int32) - 1
    to_smem = pltpu.make_async_copy(table_ref, table, table_sem)
    to_smem.start()
    to_smem.wait()

    def near(u, _):
        for r in range(2):
            rows = tile(jnp.maximum(table[r * NSEQ + u, me], 0))
            for kind, ref in ((0, k_ref), (1, v_ref)):
                pltpu.make_async_copy(ref.at[rows, pl.ds(0, HD)], send_ref.at[u, kind * 2 + r], sem).start()
        return 0

    def far(u, _):
        for r in range(2):
            rows = tile(jnp.maximum(table[r * NSEQ + NSEQ - 1 - u, NSEQ - 1 - me], 0))
            for kind in range(2):
                pltpu.make_async_copy(far_ref.at[kind, rows, :], send_ref.at[u, kind * 2 + r], sem).start()
        return 0

    lax.fori_loop(me, NSEQ, near, 0)
    lax.fori_loop(0, me, far, 0)
    pltpu.make_async_copy(send_ref, send_ref, sem).wait()


def select(where, rows, upto8, k, v, far):
    spec = lambda space: pl.BlockSpec(memory_space=space)
    return pl.pallas_call(
        select_kernel,
        name="select",
        in_specs=[spec(pltpu.SMEM)] + [spec(pltpu.VMEM)] * 5,
        out_specs=[spec(pltpu.VMEM), spec(pl.ANY)],
        out_shape=[
            jax.ShapeDtypeStruct((2 * NSEQ, NSEQ), jnp.int32),
            jax.ShapeDtypeStruct((NSEQ, 4, BLK, HD), jnp.bfloat16),
        ],
        scratch_shapes=[
            pltpu.SMEM((2 * NSEQ, NSEQ), jnp.int32),
            pltpu.SemaphoreType.DMA,
            pltpu.SemaphoreType.DMA,
        ],
        cost_estimate=pl.CostEstimate(flops=10_000_000, bytes_accessed=4 << 20, transcendentals=0),
    )(where, rows, upto8, k, v, far)


def prep_kernel(where_ref, rows_ref, upto_ref, upto8_ref, blocks_ref, *refs):
    table_ref, mask_ref, named_ref, prefix_ref, wanted_ref = refs
    me = where_ref[0]
    nid = NSEQ * 8
    bf = jnp.bfloat16
    named, wanted = names(rows_ref)
    named_ref[...] = named
    prefix = dot(wanted.astype(bf), upto_ref[...], NN)
    prefix8 = dot(wanted.astype(bf), upto8_ref[...], NN)
    ones = flag(owners()[0]).astype(bf)
    table_ref[0 : 2 * NSEQ, :] = blocks_ref[...]
    for r in range(2):
        picked = jnp.where(prefix8 == float(r + 1), wanted, 0.0)
        place = dot((picked * (prefix - 1.0)).astype(bf), ones, NN)
        spare = iota((NSEQ, NSEQ), 1) + POOL + NSEQ * r
        has = blocks_ref[r * NSEQ : (r + 1) * NSEQ, :] >= 0
        table_ref[(2 + r) * NSEQ : (3 + r) * NSEQ, :] = jnp.where(has, place.astype(jnp.int32), spare)
    prefix_ref[...] = jnp.where(wanted > 0.5, prefix - 1.0, -1.0)
    wanted_ref[...] = wanted
    spread = flag(iota((8, SEG), 0) == (iota((8, SEG), 1) >> 6))
    ids8, row8 = iota((8, nid), 1), iota((8, nid), 0)
    for h in range(2):
        seg = me if h == 0 else NSEQ - 1 - me
        compact = flag(iota((POOL, nid), 0).astype(jnp.float32) == prefix_ref[pl.ds(seg, 1), :])
        used = jnp.where(ids8 < seg * 8 + row8, named_ref[pl.ds(pl.multiple_of(seg * 8, 8), 8), :], 0.0)
        by_id = dot(used.astype(bf), spread.astype(bf), TN)
        mask_ref[h] = dot(compact.astype(bf), by_id.astype(bf), NN)
        held = jnp.where(iota((1, nid), 1) < seg * 8 + 8, wanted_ref[pl.ds(seg, 1), :], 0.0)
        count = jnp.sum(held, axis=1, keepdims=True)
        table_ref[COUNT_ROW + h : COUNT_ROW + h + 1, :] = jnp.broadcast_to(count, (1, NSEQ)).astype(jnp.int32)


def prep(where, rows, upto, upto8, blocks):
    nid = NSEQ * 8
    return pl.pallas_call(
        prep_kernel,
        name="prep",
        in_specs=[pl.BlockSpec(memory_space=pltpu.SMEM)] + [pl.BlockSpec(memory_space=pltpu.VMEM)] * 4,
        out_specs=[pl.BlockSpec(memory_space=pltpu.VMEM)] * 2,
        out_shape=[
            jax.ShapeDtypeStruct((TABLE_ROWS, NSEQ), jnp.int32),
            jax.ShapeDtypeStruct((2, POOL, SEG), jnp.float32),
        ],
        scratch_shapes=[
            pltpu.VMEM((nid, nid), jnp.float32),
            pltpu.VMEM((NSEQ, nid), jnp.float32),
            pltpu.VMEM((NSEQ, nid), jnp.float32),
        ],
        cost_estimate=pl.CostEstimate(flops=10_000_000, bytes_accessed=1 << 20, transcendentals=0),
    )(where, rows, upto, upto8, blocks)


def attend_kernel(where_ref, table_ref, bias_ref, *refs):
    q_ref, do_ref, k_ref, v_ref, far_kv_ref, far_q_ref, mask_ref, got_ref = refs[:8]
    outs, back_ref = refs[8:16], refs[16]
    kt, vt, s_ref, dp_ref, add_ref, dka, dva, dkb, dvb, sems, out_sem = refs[17:]
    me = where_ref[0]
    keys = POOL * BLK
    tiles = (kt, vt)
    segs = (me, NSEQ - 1 - me)

    def fetch(u, _):
        first = u < me
        h = jnp.where(first, 0, 1)
        seg = jnp.where(first, segs[0], segs[1])
        writer = jnp.where(first, u, NSEQ - 1 - u)

        @pl.when(u != me)
        def _():
            for r in range(2):
                at = tile(h * TILES + table_ref[(2 + r) * NSEQ + seg, writer])
                for kind in range(2):
                    pltpu.make_async_copy(
                        got_ref.at[u, kind * 2 + r], tiles[kind].at[at, :], sems.at[kind]
                    ).start()

        return 0

    lax.fori_loop(0, NSEQ, fetch, 0, unroll=4)
    heads = []
    for h in range(2):
        if h == 0:
            lanes = slice(0, HD)
            q, do, k, v = (r.at[:, lanes] for r in (q_ref, do_ref, k_ref, v_ref))
        else:
            q, do, k, v = far_q_ref.at[0], far_q_ref.at[1], far_kv_ref.at[0], far_kv_ref.at[1]
        heads.append((q, do, k, v))
        held = table_ref[COUNT_ROW + h, 0]
        for r in range(2):
            rows = tile(jnp.maximum(table_ref[r * NSEQ + segs[h], segs[h]], 0))
            at = tile(h * TILES + table_ref[(2 + r) * NSEQ + segs[h], segs[h]])
            kt[at, :] = k[rows, :]
            vt[at, :] = v[rows, :]

        def clear(i, _):
            at = tile(h * TILES + i)
            kt[at, :] = jnp.zeros((BLK, HD), jnp.bfloat16)
            vt[at, :] = jnp.zeros((BLK, HD), jnp.bfloat16)
            return 0

        lax.fori_loop(held, (held + SPC - 1) // SPC * SPC, clear, 0)
        for i in range(POOL // SPC):
            add_ref[h, i] = jnp.where(mask_ref[h, i * SPC : (i + 1) * SPC, :] > 0.5, bias_ref[h] * LOG2E, -1e30)

    def fold(value, op):
        return op(value.reshape(KC // 8, 8, value.shape[1]), axis=0)

    def merge(total, value, op):
        lo = total.shape[1] - value.shape[1]
        late = op(total[:, lo:], value)
        return late if lo == 0 else jnp.concatenate([total[:, :lo], late], axis=1)

    for h in range(2):
        q, do, k, v = heads[h]
        att_ref, gq_ref, dkl_ref, dvl_ref = outs[h * 4 : h * 4 + 4]
        steps = (table_ref[COUNT_ROW + h, 0] + SPC - 1) // SPC
        qc, doc = q[...], do[...]

        def chunk(i):
            return pl.ds(pl.multiple_of(i * KC, KC), KC)

        def held_chunk(i):
            return pl.ds(pl.multiple_of(h * TILES * BLK + i * KC, KC), KC)

        def mem_score(i, top):
            score = dot(kt[held_chunk(i), :], qc, NT) * (SCALE * LOG2E)
            add = add_ref[h, i]
            score = (score.reshape(SPC, BLK, QT) + add[:, None, :]).reshape(KC, QT)
            s_ref[chunk(i), :] = score
            return jnp.maximum(top, fold(score, jnp.max))

        top = jnp.full((8, QT), -1e30, jnp.float32)
        for n in range(SEG // KC):
            lo = n * KC
            score = dot(k[lo : lo + KC, :], qc[lo:], NT) * (SCALE * LOG2E)
            score = jnp.where(iota(score.shape, 0) <= iota(score.shape, 1), score, -1e30)
            s_ref[keys + lo : keys + lo + KC, lo:] = score
            top = merge(top, fold(score, jnp.max), jnp.maximum)
        if h == 0:
            for kind in range(2):
                most = tiles[kind].at[pl.ds(0, 2 * (NSEQ - 1) * BLK), :]
                pltpu.make_async_copy(most, most, sems.at[kind]).wait()
        top = lax.fori_loop(0, steps, mem_score, top)
        top = jnp.max(top, axis=0, keepdims=True)

        def weigh(i, mass):
            e = jnp.exp2(s_ref[chunk(i), :] - top)
            s_ref[chunk(i), :] = e
            return mass + fold(e, jnp.sum)

        mass = lax.fori_loop(0, steps, weigh, jnp.zeros((8, QT), jnp.float32))
        for lo in range(0, SEG, KC):
            at = slice(keys + lo, keys + lo + KC)
            e = jnp.exp2(s_ref[at, lo:] - top[:, lo:])
            s_ref[at, lo:] = e
            mass = merge(mass, fold(e, jnp.sum), jnp.add)
        inv = 1.0 / jnp.sum(mass, axis=0, keepdims=True)

        def forward(at, vc, carry, lo=0):
            out, delta = carry
            p = s_ref[at, lo:] * inv[:, lo:]
            s_ref[at, lo:] = p
            w = p.astype(jnp.bfloat16)
            out = merge(out, dot(vc, w, TN), jnp.add)
            dp = dot(vc, doc[lo:], NT)
            dp_ref[at, lo:] = dp
            return dot(w, doc[lo:], NN), (out, merge(delta, fold(p * dp, jnp.sum), jnp.add))

        def backward(at, kc, dq, lo=0):
            ds = (s_ref[at, lo:] * (dp_ref[at, lo:] - delta[:, lo:]) * SCALE).astype(jnp.bfloat16)
            return dot(ds, qc[lo:], NN), merge(dq, dot(kc, ds, TN), jnp.add)

        def mem_forward(i, carry):
            dva[chunk(i), :], carry = forward(chunk(i), vt[held_chunk(i), :], carry)
            return carry

        def mem_backward(i, dq):
            dka[chunk(i), :], dq = backward(chunk(i), kt[held_chunk(i), :], dq)
            return dq

        carry = (jnp.zeros((HD, QT), jnp.float32), jnp.zeros((8, QT), jnp.float32))
        carry = lax.fori_loop(0, steps, mem_forward, carry)
        for n in range(SEG // KC):
            rows = slice(n * KC, (n + 1) * KC)
            at = slice(keys + n * KC, keys + (n + 1) * KC)
            dvl_ref[rows, :], carry = forward(at, v[rows, :], carry, n * KC)
        out, delta = carry
        delta = jnp.sum(delta, axis=0, keepdims=True)
        att_ref[...] = out.T.astype(jnp.bfloat16)
        dq = lax.fori_loop(0, steps, mem_backward, jnp.zeros((HD, QT), jnp.float32))
        for n in range(SEG // KC):
            rows = slice(n * KC, (n + 1) * KC)
            at = slice(keys + n * KC, keys + (n + 1) * KC)
            dkl_ref[rows, :], dq = backward(at, k[rows, :], dq, n * KC)
        gq_ref[...] = dq.T.astype(jnp.bfloat16)

        def pack(i, _):
            dkb[h, chunk(i), :] = dka[chunk(i), :].astype(jnp.bfloat16)
            dvb[h, chunk(i), :] = dva[chunk(i), :].astype(jnp.bfloat16)
            return 0

        lax.fori_loop(0, steps, pack, 0)
        for r in range(2):
            block = table_ref[r * NSEQ + segs[h], segs[h]]

            @pl.when(block >= 0)
            def _():
                rows, at = tile(block), tile(table_ref[(2 + r) * NSEQ + segs[h], segs[h]])
                dkl_ref[rows, :] += dkb[h, at, :].astype(jnp.float32)
                dvl_ref[rows, :] += dvb[h, at, :].astype(jnp.float32)

        def put(u, _):
            writer = u if h == 0 else NSEQ - 1 - u
            for r in range(2):
                at = tile(jnp.minimum(table_ref[(2 + r) * NSEQ + segs[h], writer], POOL - 1))
                for kind, ref in ((0, dkb), (1, dvb)):
                    pltpu.make_async_copy(ref.at[h, at, :], back_ref.at[u, kind * 2 + r], out_sem).start()
            return 0

        lax.fori_loop(*((0, me + 1) if h == 0 else (me + 1, NSEQ)), put, 0)
    pltpu.make_async_copy(back_ref, back_ref, out_sem).wait()


def attend(where, table, bias, q, do, k, v, far_kv, far_q, mask, got):
    bf, f32, vm, hbm, sm = jnp.bfloat16, jnp.float32, pltpu.VMEM, pl.ANY, pltpu.SMEM
    spec = lambda space: pl.BlockSpec(memory_space=space)
    keys = POOL * BLK
    each = [jax.ShapeDtypeStruct((SEG, HD), d) for d in (bf, bf, f32, f32)]
    return pl.pallas_call(
        attend_kernel,
        name="attend",
        in_specs=[spec(sm)] * 3 + [spec(vm)] * 7 + [spec(hbm)],
        out_specs=[spec(vm)] * 8 + [spec(hbm)],
        out_shape=each * 2 + [jax.ShapeDtypeStruct((NSEQ, 4, BLK, HD), bf)],
        scratch_shapes=[
            pltpu.VMEM((2 * TILES * BLK, HD), bf),
            pltpu.VMEM((2 * TILES * BLK, HD), bf),
            pltpu.VMEM((keys + SEG, QT), f32),
            pltpu.VMEM((keys + SEG, QT), f32),
            pltpu.VMEM((2, POOL // SPC, SPC, SEG), f32),
            pltpu.VMEM((keys, HD), f32),
            pltpu.VMEM((keys, HD), f32),
            pltpu.VMEM((2, keys, HD), bf),
            pltpu.VMEM((2, keys, HD), bf),
            pltpu.SemaphoreType.DMA((2,)),
            pltpu.SemaphoreType.DMA,
        ],
        cost_estimate=pl.CostEstimate(flops=16_000_000_000, bytes_accessed=8 << 20, transcendentals=1_500_000),
    )(where, table, bias, q, do, k, v, far_kv, far_q, mask, got)


def settle_kernel(where_ref, table_ref, *refs):
    locals_, back_ref = refs[:4], refs[4]
    gk_ref, gv_ref, far_ref, acc = refs[5:]
    me = where_ref[0]
    part = pl.program_id(0)
    count = NSEQ // PARTS

    @pl.when(part == 0)
    def _():
        for i in range(4):
            acc[i] = locals_[i][...]

    def step(i, _):
        u = part * count + i
        first = u > me
        h = jnp.where(first, 0, 1)
        reader = jnp.where(first, u, NSEQ - 1 - u)
        writer = jnp.where(first, me, NSEQ - 1 - me)
        for r in range(2):
            block = table_ref[r * NSEQ + reader, writer]

            @pl.when((block >= 0) & (u != me))
            def _():
                for kind in range(2):
                    acc[h * 2 + kind, tile(block), :] += back_ref[i, kind * 2 + r].astype(jnp.float32)

        return 0

    lax.fori_loop(0, count, step, 0)

    @pl.when(part == PARTS - 1)
    def _():
        gk_ref[...] = acc[0].astype(jnp.bfloat16)
        gv_ref[...] = acc[1].astype(jnp.bfloat16)
        far_ref[...] = acc[2:4].astype(jnp.bfloat16)


def settle(where, table, parts, back):
    f32, bf = jnp.float32, jnp.bfloat16
    whole = lambda *shape: pl.BlockSpec(shape, lambda i, *_: (0,) * len(shape))
    return pl.pallas_call(
        settle_kernel,
        name="settle",
        grid_spec=pltpu.PrefetchScalarGridSpec(
            num_scalar_prefetch=2,
            grid=(PARTS,),
            in_specs=[whole(SEG, HD)] * 4
            + [pl.BlockSpec((NSEQ // PARTS, 4, BLK, HD), lambda i, *_: (i, 0, 0, 0))],
            out_specs=[whole(SEG, HD)] * 2 + [whole(2, SEG, HD)],
            scratch_shapes=[pltpu.VMEM((4, SEG, HD), f32)],
        ),
        out_shape=[jax.ShapeDtypeStruct((SEG, HD), bf)] * 2 + [jax.ShapeDtypeStruct((2, SEG, HD), bf)],
        compiler_params=pltpu.CompilerParams(vmem_limit_bytes=VMEM_SETTLE),
        cost_estimate=pl.CostEstimate(flops=2_000_000, bytes_accessed=3 << 20, transcendentals=0),
    )(where, table, *parts, back)


def mirror(first, second):
    pairs = [(i, NSEQ - 1 - i) for i in range(NSEQ)]
    return lax.ppermute(jnp.stack([first, second]), "seq", pairs)


def exchange(value):
    return lax.all_to_all(value, "seq", split_axis=0, concat_axis=0, tiled=True)


def layer(queries, keys, values, grad_out, retrieved, mem_bias):
    where = lax.axis_index("seq").astype(jnp.int32).reshape(1)
    devices = lax.axis_size("seq") * lax.axis_size("head")
    far_kv = mirror(keys[:, HD:], values[:, HD:])
    copies = jnp.broadcast_to(retrieved, (devices, *retrieved.shape))
    lists = lax.all_to_all(copies, ("seq", "head"), split_axis=0, concat_axis=0, tiled=True)
    far_q = mirror(queries[:, HD:], grad_out[:, HD:])
    rows = lists.reshape(devices, 16)
    row, col = iota((devices, devices), 0), iota((devices, devices), 1)
    upto = (row <= col).astype(jnp.bfloat16)
    upto8 = ((row <= col) & ((row >> 3) == (col >> 3))).astype(jnp.bfloat16)
    blocks, send = select(where, rows, upto8, keys, values, far_kv)
    table, mask = prep(where, rows, upto, upto8, blocks)
    got = exchange(send)
    att, gq, dkl, dvl, far_att, far_gq, far_dkl, far_dvl, back = attend(
        where, table, mem_bias, queries, grad_out, keys, values, far_kv, far_q, mask, got
    )
    home = mirror(far_att, far_gq)
    attended = jnp.concatenate([att, home[0]], axis=1)
    grad_queries = jnp.concatenate([gq, home[1]], axis=1)
    back = exchange(back)
    gk, gv, far = settle(where, table, (dkl, dvl, far_dkl, far_dvl), back)
    far = lax.ppermute(far, "seq", [(i, NSEQ - 1 - i) for i in range(NSEQ)])
    grad_keys = jnp.concatenate([gk, far[0]], axis=1)
    grad_values = jnp.concatenate([gv, far[1]], axis=1)
    return attended, grad_queries, grad_keys, grad_values


def solution(mesh):
    whole = P("seq", "head")
    return jax.shard_map(
        layer,
        mesh=mesh,
        in_specs=(whole, whole, whole, whole, P(("seq", "head"), None), P("head")),
        out_specs=(whole, whole, whole, whole),
        check_vma=False,
    )
```

```python
import math

import jax
import jax.numpy as jnp
from jax import lax
from jax.experimental import pallas as pl
from jax.experimental.pallas import tpu as pltpu
from jax.sharding import PartitionSpec as P


BLK = 64
NSEQ = 32
HD = 128
SEG = 512
POOL = 32
LOG2E = 1.4426950408889634
SCALE = 1.0 / math.sqrt(HD)
QT = 512
KC = 256
SPC = KC // BLK
TILES = 96
PARTS = 8
VMEM_SETTLE = 16 << 20
COUNT_ROW = 128
TABLE_ROWS = 136


def dot(a, b, dims):
    return lax.dot_general(a, b, (dims, ((), ())), preferred_element_type=jnp.float32)


NN = ((1,), (0,))
NT = ((1,), (1,))
TN = ((0,), (0,))


def iota(shape, dim):
    return lax.broadcasted_iota(jnp.int32, shape, dim)


def flag(cond):
    return jnp.where(cond, 1.0, 0.0)


def tile(index):
    return pl.ds(pl.multiple_of(index * BLK, BLK), BLK)


def names(rows_ref):
    nid = NSEQ * 8
    col = iota((nid, nid), 1)
    named = col < 0
    for e in range(16):
        named = named | (rows_ref[:, e : e + 1] == col)
    named = flag(named)
    pick = flag(iota((NSEQ, nid), 0) == (iota((NSEQ, nid), 1) >> 3)).astype(jnp.bfloat16)
    return named, flag(dot(pick, named.astype(jnp.bfloat16), NN) > 0.5)


def owners():
    gid, gw = iota((NSEQ * 8, NSEQ), 0), iota((NSEQ * 8, NSEQ), 1)
    return (gid >> 3) == gw, (gid & 7).astype(jnp.float32)


def select_kernel(where_ref, rows_ref, upto8_ref, k_ref, v_ref, far_ref, *refs):
    table_ref, send_ref, table, table_sem, sem = refs
    me = where_ref[0]
    bf = jnp.bfloat16
    _, wanted = names(rows_ref)
    prefix8 = dot(wanted.astype(bf), upto8_ref[...], NN)
    same, inner = owners()
    inner = jnp.where(same, inner + 1.0, 0.0).astype(bf)
    for r in range(2):
        picked = jnp.where(prefix8 == float(r + 1), wanted, 0.0)
        table_ref[r * NSEQ : (r + 1) * NSEQ, :] = dot(picked.astype(bf), inner, NN).astype(jnp.int32) - 1
    to_smem = pltpu.make_async_copy(table_ref, table, table_sem)
    to_smem.start()
    to_smem.wait()

    def near(u, _):
        for r in range(2):
            rows = tile(jnp.maximum(table[r * NSEQ + u, me], 0))
            for kind, ref in ((0, k_ref), (1, v_ref)):
                pltpu.make_async_copy(ref.at[rows, pl.ds(0, HD)], send_ref.at[u, kind * 2 + r], sem).start()
        return 0

    def far(u, _):
        for r in range(2):
            rows = tile(jnp.maximum(table[r * NSEQ + NSEQ - 1 - u, NSEQ - 1 - me], 0))
            for kind in range(2):
                pltpu.make_async_copy(far_ref.at[kind, rows, :], send_ref.at[u, kind * 2 + r], sem).start()
        return 0

    lax.fori_loop(me, NSEQ, near, 0)
    lax.fori_loop(0, me, far, 0)
    pltpu.make_async_copy(send_ref, send_ref, sem).wait()


def select(where, rows, upto8, k, v, far):
    spec = lambda space: pl.BlockSpec(memory_space=space)
    return pl.pallas_call(
        select_kernel,
        name="select",
        in_specs=[spec(pltpu.SMEM)] + [spec(pltpu.VMEM)] * 5,
        out_specs=[spec(pltpu.VMEM), spec(pl.ANY)],
        out_shape=[
            jax.ShapeDtypeStruct((2 * NSEQ, NSEQ), jnp.int32),
            jax.ShapeDtypeStruct((NSEQ, 4, BLK, HD), jnp.bfloat16),
        ],
        scratch_shapes=[
            pltpu.SMEM((2 * NSEQ, NSEQ), jnp.int32),
            pltpu.SemaphoreType.DMA,
            pltpu.SemaphoreType.DMA,
        ],
        cost_estimate=pl.CostEstimate(flops=10_000_000, bytes_accessed=4 << 20, transcendentals=0),
    )(where, rows, upto8, k, v, far)


def prep_kernel(where_ref, rows_ref, upto_ref, upto8_ref, blocks_ref, *refs):
    table_ref, mask_ref, named_ref, prefix_ref, wanted_ref = refs
    me = where_ref[0]
    nid = NSEQ * 8
    bf = jnp.bfloat16
    named, wanted = names(rows_ref)
    named_ref[...] = named
    prefix = dot(wanted.astype(bf), upto_ref[...], NN)
    prefix8 = dot(wanted.astype(bf), upto8_ref[...], NN)
    ones = flag(owners()[0]).astype(bf)
    table_ref[0 : 2 * NSEQ, :] = blocks_ref[...]
    for r in range(2):
        picked = jnp.where(prefix8 == float(r + 1), wanted, 0.0)
        place = dot((picked * (prefix - 1.0)).astype(bf), ones, NN)
        spare = iota((NSEQ, NSEQ), 1) + POOL + NSEQ * r
        has = blocks_ref[r * NSEQ : (r + 1) * NSEQ, :] >= 0
        table_ref[(2 + r) * NSEQ : (3 + r) * NSEQ, :] = jnp.where(has, place.astype(jnp.int32), spare)
    prefix_ref[...] = jnp.where(wanted > 0.5, prefix - 1.0, -1.0)
    wanted_ref[...] = wanted
    spread = flag(iota((8, SEG), 0) == (iota((8, SEG), 1) >> 6))
    ids8, row8 = iota((8, nid), 1), iota((8, nid), 0)
    for h in range(2):
        seg = me if h == 0 else NSEQ - 1 - me
        compact = flag(iota((POOL, nid), 0).astype(jnp.float32) == prefix_ref[pl.ds(seg, 1), :])
        used = jnp.where(ids8 < seg * 8 + row8, named_ref[pl.ds(pl.multiple_of(seg * 8, 8), 8), :], 0.0)
        by_id = dot(used.astype(bf), spread.astype(bf), TN)
        mask_ref[h] = dot(compact.astype(bf), by_id.astype(bf), NN)
        held = jnp.where(iota((1, nid), 1) < seg * 8 + 8, wanted_ref[pl.ds(seg, 1), :], 0.0)
        count = jnp.sum(held, axis=1, keepdims=True)
        table_ref[COUNT_ROW + h : COUNT_ROW + h + 1, :] = jnp.broadcast_to(count, (1, NSEQ)).astype(jnp.int32)


def prep(where, rows, upto, upto8, blocks):
    nid = NSEQ * 8
    return pl.pallas_call(
        prep_kernel,
        name="prep",
        in_specs=[pl.BlockSpec(memory_space=pltpu.SMEM)] + [pl.BlockSpec(memory_space=pltpu.VMEM)] * 4,
        out_specs=[pl.BlockSpec(memory_space=pltpu.VMEM)] * 2,
        out_shape=[
            jax.ShapeDtypeStruct((TABLE_ROWS, NSEQ), jnp.int32),
            jax.ShapeDtypeStruct((2, POOL, SEG), jnp.float32),
        ],
        scratch_shapes=[
            pltpu.VMEM((nid, nid), jnp.float32),
            pltpu.VMEM((NSEQ, nid), jnp.float32),
            pltpu.VMEM((NSEQ, nid), jnp.float32),
        ],
        cost_estimate=pl.CostEstimate(flops=10_000_000, bytes_accessed=1 << 20, transcendentals=0),
    )(where, rows, upto, upto8, blocks)


def attend_kernel(h, where_ref, table_ref, bias_ref, q_ref, do_ref, k_ref, v_ref, mask_ref, got_ref, *refs):
    refs = refs[1 - h :]
    (att_ref, gq_ref, dkl_ref, dvl_ref), back_ref = refs[:4], refs[4]
    kt, vt, s_ref, dp_ref, add_ref, dka, dva, dkb, dvb, sems, out_sem = refs[5:]
    me = where_ref[0]
    keys = POOL * BLK
    tiles = (kt, vt)
    seg = me if h == 0 else NSEQ - 1 - me
    first, last = (0, me) if h == 0 else (me + 1, NSEQ)

    def fetch(u, _):
        writer = u if h == 0 else NSEQ - 1 - u
        for r in range(2):
            at = tile(table_ref[(2 + r) * NSEQ + seg, writer])
            for kind in range(2):
                pltpu.make_async_copy(got_ref.at[u, kind * 2 + r], tiles[kind].at[at, :], sems.at[kind]).start()
        return 0

    def fetched(u, _):
        for kind in range(2):
            two = tiles[kind].at[pl.ds(0, 2 * BLK), :]
            pltpu.make_async_copy(two, two, sems.at[kind]).wait()
        return 0

    lax.fori_loop(first, last, fetch, 0)
    if h == 0:
        q, do, k, v = (r.at[:, pl.ds(0, HD)] for r in (q_ref, do_ref, k_ref, v_ref))
    else:
        q, do, k, v = (r.at[0] for r in (q_ref, do_ref, k_ref, v_ref))
    held = table_ref[COUNT_ROW + h, 0]
    for r in range(2):
        rows = tile(jnp.maximum(table_ref[r * NSEQ + seg, seg], 0))
        at = tile(table_ref[(2 + r) * NSEQ + seg, seg])
        kt[at, :] = k[rows, :]
        vt[at, :] = v[rows, :]

    def clear(i, _):
        kt[tile(i), :] = jnp.zeros((BLK, HD), jnp.bfloat16)
        vt[tile(i), :] = jnp.zeros((BLK, HD), jnp.bfloat16)
        return 0

    lax.fori_loop(held, (held + SPC - 1) // SPC * SPC, clear, 0)
    for i in range(POOL // SPC):
        add_ref[i] = jnp.where(mask_ref[h, i * SPC : (i + 1) * SPC, :] > 0.5, bias_ref[h] * LOG2E, -1e30)

    def fold(value, op):
        return op(value.reshape(KC // 8, 8, value.shape[1]), axis=0)

    def merge(total, value, op):
        lo = total.shape[1] - value.shape[1]
        late = op(total[:, lo:], value)
        return late if lo == 0 else jnp.concatenate([total[:, :lo], late], axis=1)

    steps = (held + SPC - 1) // SPC
    qc, doc = q[...], do[...]

    def chunk(i):
        return pl.ds(pl.multiple_of(i * KC, KC), KC)

    def mem_score(i, top):
        score = dot(kt[chunk(i), :], qc, NT) * (SCALE * LOG2E)
        add = add_ref[i]
        score = (score.reshape(SPC, BLK, QT) + add[:, None, :]).reshape(KC, QT)
        s_ref[chunk(i), :] = score
        return jnp.maximum(top, fold(score, jnp.max))

    top = jnp.full((8, QT), -1e30, jnp.float32)
    for n in range(SEG // KC):
        lo = n * KC
        score = dot(k[lo : lo + KC, :], qc[lo:], NT) * (SCALE * LOG2E)
        score = jnp.where(iota(score.shape, 0) <= iota(score.shape, 1), score, -1e30)
        s_ref[keys + lo : keys + lo + KC, lo:] = score
        top = merge(top, fold(score, jnp.max), jnp.maximum)
    lax.fori_loop(first, last, fetched, 0)
    top = lax.fori_loop(0, steps, mem_score, top)
    top = jnp.max(top, axis=0, keepdims=True)

    def weigh(i, mass):
        e = jnp.exp2(s_ref[chunk(i), :] - top)
        s_ref[chunk(i), :] = e
        return mass + fold(e, jnp.sum)

    mass = lax.fori_loop(0, steps, weigh, jnp.zeros((8, QT), jnp.float32))
    for lo in range(0, SEG, KC):
        at = slice(keys + lo, keys + lo + KC)
        e = jnp.exp2(s_ref[at, lo:] - top[:, lo:])
        s_ref[at, lo:] = e
        mass = merge(mass, fold(e, jnp.sum), jnp.add)
    inv = 1.0 / jnp.sum(mass, axis=0, keepdims=True)

    def forward(at, vc, carry, lo=0):
        out, delta = carry
        p = s_ref[at, lo:] * inv[:, lo:]
        s_ref[at, lo:] = p
        w = p.astype(jnp.bfloat16)
        out = merge(out, dot(vc, w, TN), jnp.add)
        dp = dot(vc, doc[lo:], NT)
        dp_ref[at, lo:] = dp
        return dot(w, doc[lo:], NN), (out, merge(delta, fold(p * dp, jnp.sum), jnp.add))

    def backward(at, kc, dq, lo=0):
        ds = (s_ref[at, lo:] * (dp_ref[at, lo:] - delta[:, lo:]) * SCALE).astype(jnp.bfloat16)
        return dot(ds, qc[lo:], NN), merge(dq, dot(kc, ds, TN), jnp.add)

    def mem_forward(i, carry):
        dva[chunk(i), :], carry = forward(chunk(i), vt[chunk(i), :], carry)
        return carry

    def mem_backward(i, dq):
        dka[chunk(i), :], dq = backward(chunk(i), kt[chunk(i), :], dq)
        return dq

    carry = (jnp.zeros((HD, QT), jnp.float32), jnp.zeros((8, QT), jnp.float32))
    carry = lax.fori_loop(0, steps, mem_forward, carry)
    for n in range(SEG // KC):
        rows = slice(n * KC, (n + 1) * KC)
        at = slice(keys + n * KC, keys + (n + 1) * KC)
        dvl_ref[rows, :], carry = forward(at, v[rows, :], carry, n * KC)
    out, delta = carry
    delta = jnp.sum(delta, axis=0, keepdims=True)
    att_ref[...] = out.T.astype(jnp.bfloat16)
    dq = lax.fori_loop(0, steps, mem_backward, jnp.zeros((HD, QT), jnp.float32))
    for n in range(SEG // KC):
        rows = slice(n * KC, (n + 1) * KC)
        at = slice(keys + n * KC, keys + (n + 1) * KC)
        dkl_ref[rows, :], dq = backward(at, k[rows, :], dq, n * KC)
    gq_ref[...] = dq.T.astype(jnp.bfloat16)

    def pack(i, _):
        dkb[chunk(i), :] = dka[chunk(i), :].astype(jnp.bfloat16)
        dvb[chunk(i), :] = dva[chunk(i), :].astype(jnp.bfloat16)
        return 0

    lax.fori_loop(0, steps, pack, 0)
    for r in range(2):
        block = table_ref[r * NSEQ + seg, seg]

        @pl.when(block >= 0)
        def _():
            rows, at = tile(block), tile(table_ref[(2 + r) * NSEQ + seg, seg])
            dkl_ref[rows, :] += dkb[at, :].astype(jnp.float32)
            dvl_ref[rows, :] += dvb[at, :].astype(jnp.float32)

    def put(u, _):
        writer = u if h == 0 else NSEQ - 1 - u
        for r in range(2):
            at = tile(jnp.minimum(table_ref[(2 + r) * NSEQ + seg, writer], POOL - 1))
            for kind, ref in ((0, dkb), (1, dvb)):
                pltpu.make_async_copy(ref.at[at, :], back_ref.at[u, kind * 2 + r], out_sem).start()
        return 0

    def sent(u, _):
        pltpu.make_async_copy(back_ref.at[0], back_ref.at[0], out_sem).wait()
        return 0

    ends = (0, me + 1) if h == 0 else (me + 1, NSEQ)
    lax.fori_loop(*ends, put, 0)
    lax.fori_loop(*ends, sent, 0)


def attend(h, where, table, bias, q, do, k, v, mask, got, back=()):
    bf, f32, vm, hbm, sm = jnp.bfloat16, jnp.float32, pltpu.VMEM, pl.ANY, pltpu.SMEM
    spec = lambda space: pl.BlockSpec(memory_space=space)
    keys = POOL * BLK
    if h == 0:
        ins = [spec(vm)] * 4
    else:
        half = lambda i: pl.BlockSpec((1, SEG, HD), lambda _: (i, 0, 0))
        ins = [half(0), half(1), half(0), half(1)]
    return pl.pallas_call(
        lambda *refs: attend_kernel(h, *refs),
        grid=(1,) if h else (),
        in_specs=[spec(sm)] * 3 + ins + [spec(vm), spec(hbm)] + [spec(hbm)] * len(back),
        out_specs=[spec(vm)] * 4 + [spec(hbm)],
        out_shape=[jax.ShapeDtypeStruct((SEG, HD), d) for d in (bf, bf, f32, f32)]
        + [jax.ShapeDtypeStruct((NSEQ, 4, BLK, HD), bf)],
        scratch_shapes=[
            pltpu.VMEM((TILES * BLK, HD), bf),
            pltpu.VMEM((TILES * BLK, HD), bf),
            pltpu.VMEM((keys + SEG, QT), f32),
            pltpu.VMEM((keys + SEG, QT), f32),
            pltpu.VMEM((POOL // SPC, SPC, SEG), f32),
            pltpu.VMEM((keys, HD), f32),
            pltpu.VMEM((keys, HD), f32),
            pltpu.VMEM((keys, HD), bf),
            pltpu.VMEM((keys, HD), bf),
            pltpu.SemaphoreType.DMA((2,)),
            pltpu.SemaphoreType.DMA,
        ],
        input_output_aliases={9: 4} if back else {},
        cost_estimate=pl.CostEstimate(flops=8_000_000_000, bytes_accessed=4 << 20, transcendentals=750_000),
    )(where, table, bias, q, do, k, v, mask, got, *back)


def settle_kernel(where_ref, table_ref, *refs):
    locals_, back_ref = refs[:4], refs[4]
    gk_ref, gv_ref, far_ref, acc = refs[5:]
    me = where_ref[0]
    part = pl.program_id(0)
    count = NSEQ // PARTS

    @pl.when(part == 0)
    def _():
        for i in range(4):
            acc[i] = locals_[i][...]

    def step(i, _):
        u = part * count + i
        first = u > me
        h = jnp.where(first, 0, 1)
        reader = jnp.where(first, u, NSEQ - 1 - u)
        writer = jnp.where(first, me, NSEQ - 1 - me)
        for r in range(2):
            block = table_ref[r * NSEQ + reader, writer]

            @pl.when((block >= 0) & (u != me))
            def _():
                for kind in range(2):
                    acc[h * 2 + kind, tile(block), :] += back_ref[i, kind * 2 + r].astype(jnp.float32)

        return 0

    lax.fori_loop(0, count, step, 0)

    @pl.when(part == PARTS - 1)
    def _():
        gk_ref[...] = acc[0].astype(jnp.bfloat16)
        gv_ref[...] = acc[1].astype(jnp.bfloat16)
        far_ref[...] = acc[2:4].astype(jnp.bfloat16)


def settle(where, table, parts, back):
    f32, bf = jnp.float32, jnp.bfloat16
    whole = lambda *shape: pl.BlockSpec(shape, lambda i, *_: (0,) * len(shape))
    return pl.pallas_call(
        settle_kernel,
        name="settle",
        grid_spec=pltpu.PrefetchScalarGridSpec(
            num_scalar_prefetch=2,
            grid=(PARTS,),
            in_specs=[whole(SEG, HD)] * 4
            + [pl.BlockSpec((NSEQ // PARTS, 4, BLK, HD), lambda i, *_: (i, 0, 0, 0))],
            out_specs=[whole(SEG, HD)] * 2 + [whole(2, SEG, HD)],
            scratch_shapes=[pltpu.VMEM((4, SEG, HD), f32)],
        ),
        out_shape=[jax.ShapeDtypeStruct((SEG, HD), bf)] * 2 + [jax.ShapeDtypeStruct((2, SEG, HD), bf)],
        compiler_params=pltpu.CompilerParams(vmem_limit_bytes=VMEM_SETTLE),
        cost_estimate=pl.CostEstimate(flops=2_000_000, bytes_accessed=3 << 20, transcendentals=0),
    )(where, table, *parts, back)


def mirror(first, second):
    pairs = [(i, NSEQ - 1 - i) for i in range(NSEQ)]
    return lax.ppermute(jnp.stack([first, second]), "seq", pairs)


def exchange(value):
    return lax.all_to_all(value, "seq", split_axis=0, concat_axis=0, tiled=True)


def layer(queries, keys, values, grad_out, retrieved, mem_bias):
    where = lax.axis_index("seq").astype(jnp.int32).reshape(1)
    devices = lax.axis_size("seq") * lax.axis_size("head")
    far_kv = mirror(keys[:, HD:], values[:, HD:])
    copies = jnp.broadcast_to(retrieved, (devices, *retrieved.shape))
    lists = lax.all_to_all(copies, ("seq", "head"), split_axis=0, concat_axis=0, tiled=True)
    far_q = mirror(queries[:, HD:], grad_out[:, HD:])
    rows = lists.reshape(devices, 16)
    row, col = iota((devices, devices), 0), iota((devices, devices), 1)
    upto = (row <= col).astype(jnp.bfloat16)
    upto8 = ((row <= col) & ((row >> 3) == (col >> 3))).astype(jnp.bfloat16)
    blocks, send = select(where, rows, upto8, keys, values, far_kv)
    table, mask = prep(where, rows, upto, upto8, blocks)
    got = exchange(send)
    far_att, far_gq, far_dkl, far_dvl, back = attend(
        1, where, table, mem_bias, far_q, far_q, far_kv, far_kv, mask, got
    )
    att, gq, dkl, dvl, back = attend(
        0, where, table, mem_bias, queries, grad_out, keys, values, mask, got, (back,)
    )
    home = mirror(far_att, far_gq)
    attended = jnp.concatenate([att, home[0]], axis=1)
    grad_queries = jnp.concatenate([gq, home[1]], axis=1)
    back = exchange(back)
    gk, gv, far = settle(where, table, (dkl, dvl, far_dkl, far_dvl), back)
    far = lax.ppermute(far, "seq", [(i, NSEQ - 1 - i) for i in range(NSEQ)])
    grad_keys = jnp.concatenate([gk, far[0]], axis=1)
    grad_values = jnp.concatenate([gv, far[1]], axis=1)
    return attended, grad_queries, grad_keys, grad_values


def solution(mesh):
    whole = P("seq", "head")
    return jax.shard_map(
        layer,
        mesh=mesh,
        in_specs=(whole, whole, whole, whole, P(("seq", "head"), None), P("head")),
        out_specs=(whole, whole, whole, whole),
        check_vma=False,
    )
```

```python
import math

import jax
import jax.numpy as jnp
from jax import lax
from jax.experimental import pallas as pl
from jax.experimental.pallas import tpu as pltpu
from jax.sharding import PartitionSpec as P


BLK = 64
NSEQ = 32
HD = 128
FEAT = 256
SEG = 512
POOL = 32
LOG2E = 1.4426950408889634
SCALE = 1.0 / math.sqrt(HD)
QT = 512
KC = 256
SPC = KC // BLK
TILES = 96
PARTS = 8
VMEM_SETTLE = 16 << 20
COUNT_ROW = 128
TABLE_ROWS = 136


def dot(a, b, dims):
    return lax.dot_general(a, b, (dims, ((), ())), preferred_element_type=jnp.float32)


NN = ((1,), (0,))
NT = ((1,), (1,))
TN = ((0,), (0,))


def iota(shape, dim):
    return lax.broadcasted_iota(jnp.int32, shape, dim)


def flag(cond):
    return jnp.where(cond, 1.0, 0.0)


def tile(index):
    return pl.ds(pl.multiple_of(index * BLK, BLK), BLK)


def names(rows_ref):
    nid = NSEQ * 8
    col = iota((nid, nid), 1)
    named = col < 0
    for e in range(16):
        named = named | (rows_ref[:, e : e + 1] == col)
    named = flag(named)
    pick = flag(iota((NSEQ, nid), 0) == (iota((NSEQ, nid), 1) >> 3)).astype(jnp.bfloat16)
    return named, flag(dot(pick, named.astype(jnp.bfloat16), NN) > 0.5)


def owners():
    gid, gw = iota((NSEQ * 8, NSEQ), 0), iota((NSEQ * 8, NSEQ), 1)
    return (gid >> 3) == gw, (gid & 7).astype(jnp.float32)


def select_kernel(where_ref, rows_ref, upto8_ref, k_ref, v_ref, far_ref, *refs):
    table_ref, send_ref, table, table_sem, sem = refs
    me = where_ref[0]
    bf = jnp.bfloat16
    _, wanted = names(rows_ref)
    prefix8 = dot(wanted.astype(bf), upto8_ref[...], NN)
    same, inner = owners()
    inner = jnp.where(same, inner + 1.0, 0.0).astype(bf)
    for r in range(2):
        picked = jnp.where(prefix8 == float(r + 1), wanted, 0.0)
        table_ref[r * NSEQ : (r + 1) * NSEQ, :] = dot(picked.astype(bf), inner, NN).astype(jnp.int32) - 1
    to_smem = pltpu.make_async_copy(table_ref, table, table_sem)
    to_smem.start()
    to_smem.wait()

    def near(u, _):
        for r in range(2):
            rows = tile(jnp.maximum(table[r * NSEQ + u, me], 0))
            for kind, ref in ((0, k_ref), (1, v_ref)):
                pltpu.make_async_copy(ref.at[rows, pl.ds(0, HD)], send_ref.at[u, kind * 2 + r], sem).start()
        return 0

    def far(u, _):
        for r in range(2):
            rows = tile(jnp.maximum(table[r * NSEQ + NSEQ - 1 - u, NSEQ - 1 - me], 0))
            for kind in range(2):
                pltpu.make_async_copy(far_ref.at[kind, rows, :], send_ref.at[u, kind * 2 + r], sem).start()
        return 0

    lax.fori_loop(me, NSEQ, near, 0)
    lax.fori_loop(0, me, far, 0)
    pltpu.make_async_copy(send_ref, send_ref, sem).wait()


def select(where, rows, upto8, k, v, far):
    spec = lambda space: pl.BlockSpec(memory_space=space)
    return pl.pallas_call(
        select_kernel,
        name="select",
        in_specs=[spec(pltpu.SMEM)] + [spec(pltpu.VMEM)] * 5,
        out_specs=[spec(pltpu.VMEM), spec(pl.ANY)],
        out_shape=[
            jax.ShapeDtypeStruct((2 * NSEQ, NSEQ), jnp.int32),
            jax.ShapeDtypeStruct((NSEQ, 4, BLK, HD), jnp.bfloat16),
        ],
        scratch_shapes=[
            pltpu.SMEM((2 * NSEQ, NSEQ), jnp.int32),
            pltpu.SemaphoreType.DMA,
            pltpu.SemaphoreType.DMA,
        ],
        cost_estimate=pl.CostEstimate(flops=10_000_000, bytes_accessed=4 << 20, transcendentals=0),
    )(where, rows, upto8, k, v, far)


def prep_kernel(where_ref, rows_ref, upto_ref, upto8_ref, blocks_ref, *refs):
    table_ref, mask_ref, named_ref, prefix_ref, wanted_ref = refs
    me = where_ref[0]
    nid = NSEQ * 8
    bf = jnp.bfloat16
    named, wanted = names(rows_ref)
    named_ref[...] = named
    prefix = dot(wanted.astype(bf), upto_ref[...], NN)
    prefix8 = dot(wanted.astype(bf), upto8_ref[...], NN)
    ones = flag(owners()[0]).astype(bf)
    table_ref[0 : 2 * NSEQ, :] = blocks_ref[...]
    for r in range(2):
        picked = jnp.where(prefix8 == float(r + 1), wanted, 0.0)
        place = dot((picked * (prefix - 1.0)).astype(bf), ones, NN)
        spare = iota((NSEQ, NSEQ), 1) + POOL + NSEQ * r
        has = blocks_ref[r * NSEQ : (r + 1) * NSEQ, :] >= 0
        table_ref[(2 + r) * NSEQ : (3 + r) * NSEQ, :] = jnp.where(has, place.astype(jnp.int32), spare)
    prefix_ref[...] = jnp.where(wanted > 0.5, prefix - 1.0, -1.0)
    wanted_ref[...] = wanted
    spread = flag(iota((8, SEG), 0) == (iota((8, SEG), 1) >> 6))
    ids8, row8 = iota((8, nid), 1), iota((8, nid), 0)
    for h in range(2):
        seg = me if h == 0 else NSEQ - 1 - me
        compact = flag(iota((POOL, nid), 0).astype(jnp.float32) == prefix_ref[pl.ds(seg, 1), :])
        used = jnp.where(ids8 < seg * 8 + row8, named_ref[pl.ds(pl.multiple_of(seg * 8, 8), 8), :], 0.0)
        by_id = dot(used.astype(bf), spread.astype(bf), TN)
        mask_ref[h] = dot(compact.astype(bf), by_id.astype(bf), NN)
        held = jnp.where(iota((1, nid), 1) < seg * 8 + 8, wanted_ref[pl.ds(seg, 1), :], 0.0)
        count = jnp.sum(held, axis=1, keepdims=True)
        table_ref[COUNT_ROW + h : COUNT_ROW + h + 1, :] = jnp.broadcast_to(count, (1, NSEQ)).astype(jnp.int32)


def prep(where, rows, upto, upto8, blocks):
    nid = NSEQ * 8
    return pl.pallas_call(
        prep_kernel,
        name="prep",
        in_specs=[pl.BlockSpec(memory_space=pltpu.SMEM)] + [pl.BlockSpec(memory_space=pltpu.VMEM)] * 4,
        out_specs=[pl.BlockSpec(memory_space=pltpu.VMEM)] * 2,
        out_shape=[
            jax.ShapeDtypeStruct((TABLE_ROWS, NSEQ), jnp.int32),
            jax.ShapeDtypeStruct((2, POOL, SEG), jnp.float32),
        ],
        scratch_shapes=[
            pltpu.VMEM((nid, nid), jnp.float32),
            pltpu.VMEM((NSEQ, nid), jnp.float32),
            pltpu.VMEM((NSEQ, nid), jnp.float32),
        ],
        cost_estimate=pl.CostEstimate(flops=10_000_000, bytes_accessed=1 << 20, transcendentals=0),
    )(where, rows, upto, upto8, blocks)


def attend_kernel(where_ref, table_ref, bias_ref, *refs):
    q_ref, do_ref, k_ref, v_ref, far_kv_ref, far_q_ref, mask_ref, got_ref = refs[:8]
    outs, back_ref = refs[8:16], refs[16]
    kt, vt, s_ref, dp_ref, add_ref, dka, dva, dkb, dvb, sems, out_sem = refs[17:]
    me = where_ref[0]
    keys = POOL * BLK
    tiles = (kt, vt)
    segs = (me, NSEQ - 1 - me)

    def fetch(u, _):
        first = u < me
        h = jnp.where(first, 0, 1)
        seg = jnp.where(first, segs[0], segs[1])
        writer = jnp.where(first, u, NSEQ - 1 - u)

        @pl.when(u != me)
        def _():
            for r in range(2):
                at = tile(h * TILES + table_ref[(2 + r) * NSEQ + seg, writer])
                for kind in range(2):
                    pltpu.make_async_copy(
                        got_ref.at[u, kind * 2 + r], tiles[kind].at[at, :], sems.at[kind]
                    ).start()

        return 0

    lax.fori_loop(0, NSEQ, fetch, 0, unroll=4)
    heads = []
    for h in range(2):
        if h == 0:
            lanes = slice(0, HD)
            q, do, k, v = (r.at[:, lanes] for r in (q_ref, do_ref, k_ref, v_ref))
        else:
            q, do, k, v = far_q_ref.at[0], far_q_ref.at[1], far_kv_ref.at[0], far_kv_ref.at[1]
        heads.append((q, do, k, v))
        held = table_ref[COUNT_ROW + h, 0]
        for r in range(2):
            rows = tile(jnp.maximum(table_ref[r * NSEQ + segs[h], segs[h]], 0))
            at = tile(h * TILES + table_ref[(2 + r) * NSEQ + segs[h], segs[h]])
            kt[at, :] = k[rows, :]
            vt[at, :] = v[rows, :]

        def clear(i, _):
            at = tile(h * TILES + i)
            kt[at, :] = jnp.zeros((BLK, HD), jnp.bfloat16)
            vt[at, :] = jnp.zeros((BLK, HD), jnp.bfloat16)
            return 0

        lax.fori_loop(held, (held + SPC - 1) // SPC * SPC, clear, 0)
        for i in range(POOL // SPC):
            add_ref[h, i] = jnp.where(mask_ref[h, i * SPC : (i + 1) * SPC, :] > 0.5, bias_ref[h] * LOG2E, -1e30)

    def fold(value, op):
        return op(value.reshape(KC // 8, 8, value.shape[1]), axis=0)

    def merge(total, value, op):
        lo = total.shape[1] - value.shape[1]
        late = op(total[:, lo:], value)
        return late if lo == 0 else jnp.concatenate([total[:, :lo], late], axis=1)

    for h in range(2):
        q, do, k, v = heads[h]
        att_ref, gq_ref, dkl_ref, dvl_ref = outs[h * 4 : h * 4 + 4]
        steps = (table_ref[COUNT_ROW + h, 0] + SPC - 1) // SPC
        qc, doc = q[...], do[...]

        def chunk(i):
            return pl.ds(pl.multiple_of(i * KC, KC), KC)

        def held_chunk(i):
            return pl.ds(pl.multiple_of(h * TILES * BLK + i * KC, KC), KC)

        def mem_score(i, top):
            score = dot(kt[held_chunk(i), :], qc, NT) * (SCALE * LOG2E)
            add = add_ref[h, i]
            score = (score.reshape(SPC, BLK, QT) + add[:, None, :]).reshape(KC, QT)
            s_ref[chunk(i), :] = score
            return jnp.maximum(top, fold(score, jnp.max))

        top = jnp.full((8, QT), -1e30, jnp.float32)
        for n in range(SEG // KC):
            lo = n * KC
            score = dot(k[lo : lo + KC, :], qc[lo:], NT) * (SCALE * LOG2E)
            score = jnp.where(iota(score.shape, 0) <= iota(score.shape, 1), score, -1e30)
            s_ref[keys + lo : keys + lo + KC, lo:] = score
            top = merge(top, fold(score, jnp.max), jnp.maximum)
        if h == 0:
            for kind in range(2):
                most = tiles[kind].at[pl.ds(0, 2 * (NSEQ - 1) * BLK), :]
                pltpu.make_async_copy(most, most, sems.at[kind]).wait()
        top = lax.fori_loop(0, steps, mem_score, top)
        top = jnp.max(top, axis=0, keepdims=True)

        def weigh(i, mass):
            e = jnp.exp2(s_ref[chunk(i), :] - top)
            s_ref[chunk(i), :] = e
            return mass + fold(e, jnp.sum)

        mass = lax.fori_loop(0, steps, weigh, jnp.zeros((8, QT), jnp.float32))
        for lo in range(0, SEG, KC):
            at = slice(keys + lo, keys + lo + KC)
            e = jnp.exp2(s_ref[at, lo:] - top[:, lo:])
            s_ref[at, lo:] = e
            mass = merge(mass, fold(e, jnp.sum), jnp.add)
        inv = 1.0 / jnp.sum(mass, axis=0, keepdims=True)

        def forward(at, vc, carry, lo=0):
            out, delta = carry
            p = s_ref[at, lo:] * inv[:, lo:]
            s_ref[at, lo:] = p
            w = p.astype(jnp.bfloat16)
            out = merge(out, dot(vc, w, TN), jnp.add)
            dp = dot(vc, doc[lo:], NT)
            dp_ref[at, lo:] = dp
            return dot(w, doc[lo:], NN), (out, merge(delta, fold(p * dp, jnp.sum), jnp.add))

        def backward(at, kc, dq, lo=0):
            ds = (s_ref[at, lo:] * (dp_ref[at, lo:] - delta[:, lo:]) * SCALE).astype(jnp.bfloat16)
            return dot(ds, qc[lo:], NN), merge(dq, dot(kc, ds, TN), jnp.add)

        def mem_forward(i, carry):
            dva[chunk(i), :], carry = forward(chunk(i), vt[held_chunk(i), :], carry)
            return carry

        def mem_backward(i, dq):
            dka[chunk(i), :], dq = backward(chunk(i), kt[held_chunk(i), :], dq)
            return dq

        carry = (jnp.zeros((HD, QT), jnp.float32), jnp.zeros((8, QT), jnp.float32))
        carry = lax.fori_loop(0, steps, mem_forward, carry)
        for n in range(SEG // KC):
            rows = slice(n * KC, (n + 1) * KC)
            at = slice(keys + n * KC, keys + (n + 1) * KC)
            dvl_ref[rows, :], carry = forward(at, v[rows, :], carry, n * KC)
        out, delta = carry
        delta = jnp.sum(delta, axis=0, keepdims=True)
        att_ref[...] = out.T.astype(jnp.bfloat16)
        dq = lax.fori_loop(0, steps, mem_backward, jnp.zeros((HD, QT), jnp.float32))
        for n in range(SEG // KC):
            rows = slice(n * KC, (n + 1) * KC)
            at = slice(keys + n * KC, keys + (n + 1) * KC)
            dkl_ref[rows, :], dq = backward(at, k[rows, :], dq, n * KC)
        gq_ref[...] = dq.T.astype(jnp.bfloat16)

        def pack(i, _):
            dkb[h, chunk(i), :] = dka[chunk(i), :].astype(jnp.bfloat16)
            dvb[h, chunk(i), :] = dva[chunk(i), :].astype(jnp.bfloat16)
            return 0

        lax.fori_loop(0, steps, pack, 0)
        for r in range(2):
            block = table_ref[r * NSEQ + segs[h], segs[h]]

            @pl.when(block >= 0)
            def _():
                rows, at = tile(block), tile(table_ref[(2 + r) * NSEQ + segs[h], segs[h]])
                dkl_ref[rows, :] += dkb[h, at, :].astype(jnp.float32)
                dvl_ref[rows, :] += dvb[h, at, :].astype(jnp.float32)

        def put(u, _):
            writer = u if h == 0 else NSEQ - 1 - u
            for r in range(2):
                at = tile(jnp.minimum(table_ref[(2 + r) * NSEQ + segs[h], writer], POOL - 1))
                for kind, ref in ((0, dkb), (1, dvb)):
                    pltpu.make_async_copy(ref.at[h, at, :], back_ref.at[u, kind * 2 + r], out_sem).start()
            return 0

        lax.fori_loop(*((0, me + 1) if h == 0 else (me + 1, NSEQ)), put, 0)
    pltpu.make_async_copy(back_ref, back_ref, out_sem).wait()


def attend(where, table, bias, q, do, k, v, far_kv, far_q, mask, got):
    bf, f32, vm, hbm, sm = jnp.bfloat16, jnp.float32, pltpu.VMEM, pl.ANY, pltpu.SMEM
    spec = lambda space: pl.BlockSpec(memory_space=space)
    keys = POOL * BLK
    each = [jax.ShapeDtypeStruct((SEG, HD), d) for d in (bf, bf, f32, f32)]
    return pl.pallas_call(
        attend_kernel,
        name="attend",
        in_specs=[spec(sm)] * 3 + [spec(vm)] * 7 + [spec(hbm)],
        out_specs=[spec(vm)] * 8 + [spec(hbm)],
        out_shape=each * 2 + [jax.ShapeDtypeStruct((NSEQ, 4, BLK, HD), bf)],
        scratch_shapes=[
            pltpu.VMEM((2 * TILES * BLK, HD), bf),
            pltpu.VMEM((2 * TILES * BLK, HD), bf),
            pltpu.VMEM((keys + SEG, QT), f32),
            pltpu.VMEM((keys + SEG, QT), f32),
            pltpu.VMEM((2, POOL // SPC, SPC, SEG), f32),
            pltpu.VMEM((keys, HD), f32),
            pltpu.VMEM((keys, HD), f32),
            pltpu.VMEM((2, keys, HD), bf),
            pltpu.VMEM((2, keys, HD), bf),
            pltpu.SemaphoreType.DMA((2,)),
            pltpu.SemaphoreType.DMA,
        ],
        cost_estimate=pl.CostEstimate(flops=16_000_000_000, bytes_accessed=8 << 20, transcendentals=1_500_000),
    )(where, table, bias, q, do, k, v, far_kv, far_q, mask, got)


def settle_kernel(where_ref, table_ref, *refs):
    locals_, back_ref = refs[:4], refs[4]
    gk_ref, gv_ref, fark_ref, farv_ref, acc = refs[5:]
    me = where_ref[0]
    part = pl.program_id(0)
    count = NSEQ // PARTS

    @pl.when(part == 0)
    def _():
        for i in range(4):
            acc[i] = locals_[i][...]

    def step(i, _):
        u = part * count + i
        first = u > me
        h = jnp.where(first, 0, 1)
        reader = jnp.where(first, u, NSEQ - 1 - u)
        writer = jnp.where(first, me, NSEQ - 1 - me)
        for r in range(2):
            block = table_ref[r * NSEQ + reader, writer]

            @pl.when((block >= 0) & (u != me))
            def _():
                for kind in range(2):
                    acc[h * 2 + kind, tile(block), :] += back_ref[i, kind * 2 + r].astype(jnp.float32)

        return 0

    lax.fori_loop(0, count, step, 0)

    @pl.when(part == PARTS - 1)
    def _():
        gk_ref[:, :HD] = acc[0].astype(jnp.bfloat16)
        gv_ref[:, :HD] = acc[1].astype(jnp.bfloat16)
        fark_ref[...] = acc[2].astype(jnp.bfloat16)
        farv_ref[...] = acc[3].astype(jnp.bfloat16)


def settle(where, table, parts, back):
    f32, bf = jnp.float32, jnp.bfloat16
    whole = lambda *shape: pl.BlockSpec(shape, lambda i, *_: (0,) * len(shape))
    return pl.pallas_call(
        settle_kernel,
        name="settle",
        grid_spec=pltpu.PrefetchScalarGridSpec(
            num_scalar_prefetch=2,
            grid=(PARTS,),
            in_specs=[whole(SEG, HD)] * 4
            + [pl.BlockSpec((NSEQ // PARTS, 4, BLK, HD), lambda i, *_: (i, 0, 0, 0))],
            out_specs=[whole(SEG, FEAT)] * 2 + [whole(SEG, HD)] * 2,
            scratch_shapes=[pltpu.VMEM((4, SEG, HD), f32)],
        ),
        out_shape=[jax.ShapeDtypeStruct((SEG, FEAT), bf)] * 2 + [jax.ShapeDtypeStruct((SEG, HD), bf)] * 2,
        compiler_params=pltpu.CompilerParams(vmem_limit_bytes=VMEM_SETTLE),
        cost_estimate=pl.CostEstimate(flops=2_000_000, bytes_accessed=3 << 20, transcendentals=0),
    )(where, table, *parts, back)


def mirror(first, second):
    pairs = [(i, NSEQ - 1 - i) for i in range(NSEQ)]
    return lax.ppermute(jnp.stack([first, second]), "seq", pairs)


def exchange(value):
    return lax.all_to_all(value, "seq", split_axis=0, concat_axis=0, tiled=True)


def layer(queries, keys, values, grad_out, retrieved, mem_bias):
    where = lax.axis_index("seq").astype(jnp.int32).reshape(1)
    devices = lax.axis_size("seq") * lax.axis_size("head")
    far_kv = mirror(keys[:, HD:], values[:, HD:])
    copies = jnp.broadcast_to(retrieved, (devices, *retrieved.shape))
    lists = lax.all_to_all(copies, ("seq", "head"), split_axis=0, concat_axis=0, tiled=True)
    far_q = mirror(queries[:, HD:], grad_out[:, HD:])
    rows = lists.reshape(devices, 16)
    row, col = iota((devices, devices), 0), iota((devices, devices), 1)
    upto = (row <= col).astype(jnp.bfloat16)
    upto8 = ((row <= col) & ((row >> 3) == (col >> 3))).astype(jnp.bfloat16)
    blocks, send = select(where, rows, upto8, keys, values, far_kv)
    table, mask = prep(where, rows, upto, upto8, blocks)
    got = exchange(send)
    att, gq, dkl, dvl, far_att, far_gq, far_dkl, far_dvl, back = attend(
        where, table, mem_bias, queries, grad_out, keys, values, far_kv, far_q, mask, got
    )
    home = mirror(far_att, far_gq)
    attended = jnp.concatenate([att, home[0]], axis=1)
    grad_queries = jnp.concatenate([gq, home[1]], axis=1)
    back = exchange(back)
    gk, gv, far_gk, far_gv = settle(where, table, (dkl, dvl, far_dkl, far_dvl), back)
    pairs = [(i, NSEQ - 1 - i) for i in range(NSEQ)]
    far_gk, far_gv = (lax.ppermute(far, "seq", pairs) for far in (far_gk, far_gv))
    grad_keys = lax.dynamic_update_slice(gk, far_gk, (0, HD))
    grad_values = lax.dynamic_update_slice(gv, far_gv, (0, HD))
    return attended, grad_queries, grad_keys, grad_values


def solution(mesh):
    whole = P("seq", "head")
    return jax.shard_map(
        layer,
        mesh=mesh,
        in_specs=(whole, whole, whole, whole, P(("seq", "head"), None), P("head")),
        out_specs=(whole, whole, whole, whole),
        check_vma=False,
    )
```
